32 devices in a mesh: graph: 8 (over z, x), mp: 4 (over y, core).
Axes of the slice: x: 2, y: 2, z: 4, core: 2. Of those that a mesh axis runs over, the one named last changes fastest.
Arguments:
- features: bfloat16 [4096, 100], P('graph'), may hold values from -6 to 6
- edge_dst: int32 [4096, 4], P('graph'), may hold values from 0 to 4095, as said below
- degree: int32 [4096], P('graph'), may hold values from 1 to 20
- fresh: int32 [4096], P('graph'), may hold values 0 or 1
- seed_mask: int32 [4096], P('graph'), may hold values 0 or 1
- labels: int32 [4096], P('graph'), may hold values from 0 to 46
- table: float32 [2, 256, 4096], P(None, 'mp', 'graph'), may hold values from 0 to 1.5
- w_one: float32 [2, 100, 256], P(None, None, 'mp'), may hold values from -0.625 to 0.625
- w_two: float32 [2, 256, 256], P(None, 'mp'), may hold values from -0.375 to 0.375
- w_three: float32 [2, 256, 47], P(None, 'mp'), may hold values from -0.375 to 0.375
- m_one: float32 [2, 100, 256], P(None, None, 'mp'), may hold values from -0.01171875 to 0.01171875
- v_one: float32 [2, 100, 256], P(None, None, 'mp'), may hold values from 6.1035155e-07 to 2.4414062e-06
- m_two: float32 [2, 256, 256], P(None, 'mp'), may hold values from -0.01171875 to 0.01171875
- v_two: float32 [2, 256, 256], P(None, 'mp'), may hold values from 6.1035155e-07 to 2.4414062e-06
- m_three: float32 [2, 256, 47], P(None, 'mp'), may hold values from -0.01171875 to 0.01171875
- v_three: float32 [2, 256, 47], P(None, 'mp'), may hold values from 6.1035155e-07 to 2.4414062e-06
Outputs:
- loss: float32 [], replicated
- w_one_new: float32 [2, 100, 256], P(None, None, 'mp')
- w_two_new: float32 [2, 256, 256], P(None, 'mp')
- w_three_new: float32 [2, 256, 47], P(None, 'mp')
- w_one_copy: bfloat16 [2, 100, 256], P(None, None, 'mp')
- w_two_copy: bfloat16 [2, 256, 256], P(None, 'mp')
- w_three_copy: bfloat16 [2, 256, 47], P(None, 'mp')
- m_one_new: float32 [2, 100, 256], P(None, None, 'mp')
- m_two_new: float32 [2, 256, 256], P(None, 'mp')
- m_three_new: float32 [2, 256, 47], P(None, 'mp')
- v_one_new: float32 [2, 100, 256], P(None, None, 'mp')
- v_two_new: float32 [2, 256, 256], P(None, 'mp')
- v_three_new: float32 [2, 256, 47], P(None, 'mp')
- norms: float32 [2, 6], replicated
- table_new: float32 [2, 256, 4096], P(None, 'mp', 'graph')
The draws below stay inside these ranges and needn't reach their ends.
Inputs may be any that keep to these rules, and one draw needn't show every extreme that they name: `edge_dst`: of the edges of the 512 source rows of one index of graph, at most 512 go to the nodes of any one owner (owner = destination // 512); one owner receives exactly 512 from every index of graph.
All inputs are finite; a program needn't handle non-finite values. No bound on the sum of `fresh` or of `seed_mask` on one device may be relied on, other than what follows from the above.
Results may differ from the reference program's by a relative error of at most 0.004.
The reference program's roundings to bfloat16 on the way count: a program that leaves them out, or rounds other values in their place, can miss the bound.
Values may be sent and summed in bfloat16 or wider, within the bound.
No kernel may reach another device: no remote copies, remote signals or barrier semaphores. Data moves between devices by JAX's collectives and lax.ppermute only.
A program may use at most 64 MiB of HBM per device.

```python
import math
import jax
import jax.numpy as jnp
from jax import lax

IN = 100
HID = 256
CLS = 47
NODE_DEV = 512
FANOUT = 4
STEP = 3
NODES = 4096
CAP = 512
N_GRAPH = 8


def draw_edge_dst(key, part):
    edges = NODE_DEV * FANOUT
    half = CAP // 2
    groups = edges // half
    common = jax.random.randint(jax.random.fold_in(key, 11), (), 0, N_GRAPH)

    def one_source(source_key):
        slot_key, owner_key, row_key = jax.random.split(source_key, 3)
        slot_perm = jax.random.permutation(slot_key, edges)
        others = (common + 1 + jax.random.permutation(owner_key, N_GRAPH - 1)[:groups - 2]) % N_GRAPH
        group_owner = jnp.concatenate([jnp.stack([common, common]), others]).astype(jnp.int32)
        owner = group_owner[slot_perm // half]
        row = jax.random.randint(row_key, (edges,), 0, NODE_DEV)
        return (owner * NODE_DEV + row).astype(jnp.int32).reshape(NODE_DEV, FANOUT)
    source_keys = jax.random.split(jax.random.fold_in(key, 13), N_GRAPH)
    return jax.vmap(one_source)(source_keys).reshape(NODES, FANOUT)


def touch_ends(result, own_key, low, largest):
    dims = result.shape
    index_at = [jax.random.randint(jax.random.fold_in(own_key, axis), (), 0, dims[axis]) for axis in range(len(dims))]
    result = result.at[tuple(index_at)].set(low)
    longest = dims.index(max(dims))
    index_at[longest] = (index_at[longest] + 1) % dims[longest]
    return result.at[tuple(index_at)].set(largest)


def level_of(rng, dims, pieces, low, largest):
    factor_of, own = 1.0, jax.random.fold_in(rng, 6)
    for dim, parts in pieces:
        draws = jnp.exp(jax.random.uniform(jax.random.fold_in(own, dim), (parts,), jnp.float32, low / len(pieces), largest / len(pieces)))
        factor_of = factor_of * jnp.repeat(draws, dims[dim] // parts).reshape([-1 if axis == dim else 1 for axis in range(len(dims))])
    return factor_of


def normal_values(key, extent, spread, reach, pieces=(), kind=jnp.bfloat16):
    result = spread * jax.random.normal(key, extent, jnp.float32)
    if pieces:
        result = result * level_of(key, extent, pieces, -0.22, 0.18)
    return jnp.clip(result, -reach, reach).astype(kind)


def setup_inputs(seed: int = 0) -> dict:
    keys = jax.random.split(jax.random.key(seed), 17)
    return {
        "features": normal_values(keys[0], (NODES, IN), 1.0, 6.0, ((0, 8),)),
        "edge_dst": draw_edge_dst(jax.random.fold_in(keys[16], 71), 0),
        "degree": touch_ends(jax.random.randint(keys[2], (NODES,), 1, 21), jax.random.fold_in(keys[2], 1), 1, 20).astype(jnp.int32),
        "fresh": touch_ends((jax.random.randint(keys[3], (NODES,), 0, 4) < 3).astype(jnp.int32), jax.random.fold_in(keys[3], 1), 0, 1),
        "seed_mask": touch_ends((jax.random.randint(keys[4], (NODES,), 0, 4) < 3).astype(jnp.int32), jax.random.fold_in(keys[4], 1), 0, 1),
        "labels": touch_ends(jax.random.randint(keys[5], (NODES,), 0, CLS), jax.random.fold_in(keys[5], 1), 0, CLS - 1).astype(jnp.int32),
        "table": jnp.clip(1.5 * jax.random.uniform(keys[6], (2, HID, NODES), jnp.float32) ** level_of(keys[6], (2, HID, NODES), ((1, 4), (2, 8)), -0.2, 0.2), 0.0, 1.5),
        "w_one": normal_values(keys[7], (2, IN, HID), IN ** -0.5, 0.625, ((2, 4),), jnp.float32),
        "w_two": normal_values(keys[8], (2, HID, HID), HID ** -0.5, 0.375, ((1, 4),), jnp.float32),
        "w_three": normal_values(keys[9], (2, HID, CLS), HID ** -0.5, 0.375, ((1, 4),), jnp.float32),
        "m_one": normal_values(keys[10], (2, IN, HID), (0.05 / NODES ** 0.5), 0.01171875, ((2, 4),), jnp.float32),
        "v_one": jnp.clip(jnp.exp(math.log(2.441406195430318e-06) - 1.3862944 * jax.random.uniform(keys[11], (2, IN, HID), jnp.float32) ** level_of(keys[11], (2, IN, HID), ((2, 4),), -0.2, 0.2)), 6.103515488575795e-07, 2.441406195430318e-06),
        "m_two": normal_values(keys[12], (2, HID, HID), (0.05 / NODES ** 0.5), 0.01171875, ((1, 4),), jnp.float32),
        "v_two": jnp.clip(jnp.exp(math.log(2.441406195430318e-06) - 1.3862944 * jax.random.uniform(keys[13], (2, HID, HID), jnp.float32) ** level_of(keys[13], (2, HID, HID), ((1, 4),), -0.2, 0.2)), 6.103515488575795e-07, 2.441406195430318e-06),
        "m_three": normal_values(keys[14], (2, HID, CLS), (0.05 / NODES ** 0.5), 0.01171875, ((1, 4),), jnp.float32),
        "v_three": jnp.clip(jnp.exp(math.log(2.441406195430318e-06) - 1.3862944 * jax.random.uniform(keys[15], (2, HID, CLS), jnp.float32) ** level_of(keys[15], (2, HID, CLS), ((1, 4),), -0.2, 0.2)), 6.103515488575795e-07, 2.441406195430318e-06),
    }


@jax.custom_vjp
def low(v):
    return lax.optimization_barrier(v.astype(jnp.bfloat16)).astype(jnp.float32)

@jax.custom_vjp
def low_back(v):
    return v

def low_keep(v):
    return (low(v), None)

def low_pass(kept, grad):
    return (grad,)

def back_keep(v):
    return (v, None)

def back_low(kept, grad):
    return (low(grad),)
low.defvjp(low_keep, low_pass)
low_back.defvjp(back_keep, back_low)

def sage_layer(inputs, weights, fan_dst, degrees):
    inputs_low = low(inputs)
    weights_low = low(weights)
    own_part = jnp.dot(inputs_low, weights_low[0], precision=lax.Precision.HIGHEST)
    neighbor = low(low_back(jnp.dot(inputs_low, weights_low[1], precision=lax.Precision.HIGHEST)))
    edge_rows = jnp.repeat(neighbor, FANOUT, axis=0)
    summed = low_back(jax.ops.segment_sum(edge_rows, fan_dst, num_segments=NODES))
    return low_back(own_part + summed / degrees)

def lamb_step(weights, first, second, grad):
    correction = 1.0 - 0.5 ** STEP
    first_new = 0.5 * first + 0.5 * grad
    second_new = 0.5 * second + 0.5 * grad * grad
    update = first_new / correction / (jnp.sqrt(second_new / correction) + 1e-06) + 0.01 * weights
    weight_norm = jnp.sqrt(lax.optimization_barrier(jnp.sum(weights * weights, axis=(1, 2))))
    update_norm = jnp.sqrt(lax.optimization_barrier(jnp.sum(update * update, axis=(1, 2))))
    new_weights = weights - 0.5 * (weight_norm / update_norm)[:, None, None] * update
    return (new_weights, first_new, second_new, weight_norm, update_norm)

def reference(features, edge_dst, degree, fresh, seed_mask, labels, table, w_one, w_two, w_three, m_one, v_one, m_two, v_two, m_three, v_three):
    fan_dst = edge_dst.reshape(-1)
    degrees = degree.astype(jnp.float32)[:, None]
    is_fresh = (fresh > 0)[:, None]
    valid = seed_mask.astype(jnp.float32)
    inputs = features.astype(jnp.float32)
    targets = jax.nn.one_hot(labels, CLS, dtype=jnp.float32)

    def forward(first_w, second_w, third_w):
        hidden_one = jnp.where(is_fresh, jax.nn.relu(sage_layer(inputs, first_w, fan_dst, degrees)), table[0].T)
        hidden_two = jnp.where(is_fresh, jax.nn.relu(sage_layer(hidden_one, jnp.transpose(second_w, (0, 2, 1)), fan_dst, degrees)), table[1].T)
        logits = sage_layer(hidden_two, third_w, fan_dst, degrees)
        log_probs = jax.nn.log_softmax(logits, axis=-1)
        per_seed = -(0.9 * lax.optimization_barrier(jnp.sum(targets * log_probs, axis=-1)) + 0.1 * lax.optimization_barrier(jnp.mean(log_probs, axis=-1)))
        loss_value = jnp.sum(per_seed * valid) / jnp.sum(valid)
        return (loss_value, jnp.stack([hidden_one.T, hidden_two.T], axis=0))
    loss_value, pull_back, table_new = jax.vjp(forward, w_one, w_two, w_three, has_aux=True)
    grads = pull_back(jnp.ones((), jnp.float32))
    one_out = lamb_step(w_one, m_one, v_one, grads[0])
    two_out = lamb_step(w_two, m_two, v_two, grads[1])
    three_out = lamb_step(w_three, m_three, v_three, grads[2])
    norms = jnp.stack([jnp.concatenate([one_out[3], two_out[3], three_out[3]]), jnp.concatenate([one_out[4], two_out[4], three_out[4]])])
    return (loss_value, one_out[0], two_out[0], three_out[0], one_out[0].astype(jnp.bfloat16), two_out[0].astype(jnp.bfloat16), three_out[0].astype(jnp.bfloat16), one_out[1], two_out[1], three_out[1], one_out[2], two_out[2], three_out[2], norms, table_new)
```

```python
import jax
import jax.numpy as jnp
from jax import lax
from jax.sharding import PartitionSpec as P

STEP = 3
F32 = jnp.float32
BF16 = jnp.bfloat16
DIGIT = 256
DIRECT_MOST = 8


def nt(left, right):
    return lax.dot_general(left, right, (((1,), (1,)), ((), ())), preferred_element_type=F32)


def nn(left, right):
    return lax.dot_general(left, right, (((1,), (0,)), ((), ())), preferred_element_type=F32)


def tn(left, right):
    return lax.dot_general(left, right, (((0,), (0,)), ((), ())), preferred_element_type=F32)


def kept(value):
    return lax.reduce_precision(value, 8, 7)


def in_two(value):
    high = kept(value)
    return high.astype(BF16), (value - high).astype(BF16)


def count_block(dst_rows, first, size):
    ids = lax.broadcasted_iota(jnp.int32, (size, dst_rows.shape[1]), 0) + first
    total = (ids == dst_rows[0:1]).astype(F32)
    for slot in range(1, dst_rows.shape[0]):
        total = total + (ids == dst_rows[slot : slot + 1]).astype(F32)
    return total.astype(BF16)


def pad_rows(value, rows):
    return jnp.pad(value, ((0, rows - value.shape[0]), (0, 0)))


def pad_lanes(value, lanes):
    return jnp.pad(value, ((0, 0), (0, lanes - value.shape[1])))


def lamb_parts(weights, first, second, grad):
    correction = 1.0 - 0.5**STEP
    first_new = 0.5 * first + 0.5 * grad
    second_new = 0.5 * second + 0.5 * grad * grad
    update = first_new / correction / (jnp.sqrt(second_new / correction) + 1e-06) + 0.01 * weights
    return (first_new, second_new, update)


def local(
    features,
    edge_dst,
    degree,
    fresh,
    seed_mask,
    labels,
    table,
    w_one,
    w_two,
    w_three,
    m_one,
    v_one,
    m_two,
    v_two,
    m_three,
    v_three,
):
    devices = lax.axis_size("graph")
    me = lax.axis_index("graph")
    mine = lax.axis_index("mp")
    nodes, in_units = features.shape
    fanout = edge_dst.shape[1]
    units = w_one.shape[2]
    hidden = w_two.shape[2]
    classes = w_three.shape[2]
    direct = devices <= DIRECT_MOST and devices & (devices - 1) == 0
    degrees = degree.astype(F32)[None, :]
    is_fresh = (fresh > 0)[None, :]
    valid = seed_mask.astype(F32)[None, :]

    def gather(block):
        if not direct:
            return lax.all_gather(block, "graph", axis=1, tiled=True)
        parts = [block]
        for step in range(1, devices):
            pairs = [(i, i ^ step) for i in range(devices)]
            parts.append(lax.ppermute(block, "graph", pairs))
        return jnp.concatenate(parts, axis=1)

    def owner(step):
        return (me ^ step) if direct else step

    dst_rows = edge_dst.T
    feature_rows = features.T
    first_rows = in_units + 2 * fanout + 1
    first_message = pad_rows(
        jnp.concatenate(
            [
                feature_rows,
                (dst_rows // DIGIT).astype(BF16),
                (dst_rows % DIGIT).astype(BF16),
                valid.astype(BF16),
            ],
            axis=0,
        ),
        -(-first_rows // 16) * 16,
    )
    firsts = gather(first_message)
    low_one = jnp.transpose(w_one.astype(BF16), (0, 2, 1))
    low_two = w_two.astype(BF16)
    low_three = w_three.astype(BF16)
    wide_in = -(-in_units // 128) * 128
    wide_class = -(-classes // 64) * 64
    own_message = jnp.concatenate(
        [
            table[0].astype(BF16),
            pad_lanes(low_one[0], wide_in),
            pad_lanes(low_one[1], wide_in),
            low_two[0],
            low_two[1],
            pad_lanes(low_three[0], wide_class),
            pad_lanes(low_three[1], wide_class),
        ],
        axis=1,
    )
    whole = lax.all_gather(own_message, "mp", axis=0, tiled=True)
    cuts = [nodes, wide_in, wide_in, hidden, hidden, wide_class, wide_class]
    pieces = []
    at = 0
    for cut in cuts:
        pieces.append(whole[:, at : at + cut])
        at += cut
    old_one, all_one_self, all_one_near = pieces[0], pieces[1][:, :in_units], pieces[2][:, :in_units]
    all_two_self, all_two_near = pieces[3], pieces[4]
    all_three_self, all_three_near = pieces[5][:, :classes], pieces[6][:, :classes]

    all_features = firsts[:in_units]
    high = firsts[in_units : in_units + fanout].astype(F32)
    low = firsts[in_units + fanout : in_units + 2 * fanout].astype(F32)
    all_dst = (high * DIGIT + low).astype(jnp.int32)
    seed_count = jnp.sum(firsts[in_units + 2 * fanout].astype(F32))

    if direct:
        ahead = count_block(all_dst, me * nodes, nodes)
        back = jnp.concatenate(
            [count_block(dst_rows, owner(step) * nodes, nodes) for step in range(devices)], axis=0
        )

        def spread(all_rows):
            return nt(all_rows, ahead)

        def collect(all_rows):
            return nn(all_rows, back)

    else:

        def spread(all_rows):
            def step(total, block):
                rows = lax.dynamic_slice_in_dim(all_rows, block * nodes, nodes, 1)
                dst = lax.dynamic_slice_in_dim(all_dst, block * nodes, nodes, 1)
                return total + nt(rows, count_block(dst, me * nodes, nodes)), None

            start = jnp.zeros((all_rows.shape[0], nodes), F32)
            return lax.scan(step, start, jnp.arange(devices, dtype=jnp.int32))[0]

        def collect(all_rows):
            def step(total, block):
                rows = lax.dynamic_slice_in_dim(all_rows, block * nodes, nodes, 1)
                return total + nn(rows, count_block(dst_rows, block * nodes, nodes)), None

            start = jnp.zeros((all_rows.shape[0], nodes), F32)
            return lax.scan(step, start, jnp.arange(devices, dtype=jnp.int32))[0]

    def mine_of(rows):
        return lax.dynamic_slice_in_dim(rows, mine * units, units, 0)

    near_one = nn(all_one_near, all_features).astype(BF16)
    in_sums = spread(all_features)
    pre_one = nn(all_one_self, feature_rows) + spread(near_one) / degrees
    input_two = jnp.where(is_fresh, jax.nn.relu(pre_one).astype(BF16), old_one)
    pre_one = mine_of(pre_one)
    hidden_one = jnp.where(is_fresh, jax.nn.relu(pre_one), table[0])
    near_two = nn(low_two[1], input_two).astype(BF16)
    pre_two = nn(low_two[0], input_two) + spread(gather(near_two)) / degrees
    hidden_two = jnp.where(is_fresh, jax.nn.relu(pre_two), table[1])
    low_hidden = hidden_two.astype(BF16)
    input_three = lax.all_gather(low_hidden, "mp", axis=0, tiled=True)
    near_three = tn(all_three_near, input_three).astype(BF16)
    class_rows = -(-(classes + 1) // 16) * 16
    sums = spread(gather(pad_rows(near_three, class_rows)))[:classes]
    logits = tn(all_three_self, input_three) + sums / degrees
    log_probs = jax.nn.log_softmax(logits, axis=0)
    targets = (lax.broadcasted_iota(jnp.int32, logits.shape, 0) == labels[None, :]).astype(F32)
    per_seed = -(
        0.9 * jnp.sum(targets * log_probs, axis=0, keepdims=True)
        + 0.1 * jnp.mean(log_probs, axis=0, keepdims=True)
    )
    loss_part = jnp.sum(per_seed * valid)

    grad_logits = valid * (jnp.exp(log_probs) - 0.9 * targets - 0.1 / classes) / seed_count
    low_grad_three = grad_logits.astype(BF16)
    edge_three = (low_grad_three.astype(F32) / degrees).astype(BF16)
    lanes = lax.broadcasted_iota(jnp.int32, (1, nodes), 1)
    loss_high = kept(loss_part)
    loss_mid = kept(loss_part - loss_high)
    loss_row = jnp.where(
        lanes == 0,
        loss_high,
        jnp.where(
            lanes == 1, loss_mid, jnp.where(lanes == 2, loss_part - loss_high - loss_mid, 0.0)
        ),
    ).astype(BF16)
    thirds = gather(pad_rows(jnp.concatenate([edge_three, loss_row], axis=0), class_rows))
    loss_value = jnp.sum(thirds[classes].astype(F32)) / seed_count
    near_grad_three = collect(thirds)[:classes].astype(BF16)
    grads_three = [nt(low_hidden, low_grad_three), nt(low_hidden, near_grad_three)]
    grad_hidden_two = nn(low_three[0], low_grad_three) + nn(low_three[1], near_grad_three)
    low_grad_two = jnp.where(is_fresh & (pre_two > 0), grad_hidden_two, 0.0).astype(BF16)
    edge_two = (low_grad_two.astype(F32) / degrees).astype(BF16)
    near_grad_two = collect(gather(edge_two)).astype(BF16)
    grads_two = [nt(low_grad_two, input_two), nt(near_grad_two, input_two)]
    both = lax.all_gather(
        jnp.concatenate([low_grad_two, near_grad_two], axis=1), "mp", axis=0, tiled=True
    )
    columns_self = lax.dynamic_slice_in_dim(all_two_self, mine * units, units, 1)
    columns_near = lax.dynamic_slice_in_dim(all_two_near, mine * units, units, 1)
    grad_hidden_one = tn(columns_self, both[:, :nodes]) + tn(columns_near, both[:, nodes:])
    low_grad_one = jnp.where(is_fresh & (pre_one > 0), grad_hidden_one, 0.0).astype(BF16)
    edge_one = (low_grad_one.astype(F32) / degrees).astype(BF16)
    sums_high, sums_low = in_two(in_sums)
    grads_one = [
        nt(low_grad_one, feature_rows),
        nt(edge_one, sums_high) + nt(edge_one, sums_low),
    ]

    partial = jnp.concatenate(
        [pad_lanes(g, wide_in) for g in grads_one]
        + grads_two
        + [pad_lanes(g, wide_class) for g in grads_three],
        axis=1,
    )
    share = partial.reshape(devices, units // devices, partial.shape[1])
    share = jnp.sum(lax.all_to_all(share, "graph", 0, 0), axis=0)
    share = jnp.broadcast_to(share[None], (devices,) + share.shape)
    total = lax.all_to_all(share, "graph", 0, 0).reshape(partial.shape)
    at = 0
    pieces = []
    for cut, use in (
        (wide_in, in_units),
        (wide_in, in_units),
        (hidden, hidden),
        (hidden, hidden),
        (wide_class, classes),
        (wide_class, classes),
    ):
        pieces.append(total[:, at : at + use])
        at += cut
    grad_one = jnp.stack([pieces[0].T, pieces[1].T])
    grad_two = jnp.stack(pieces[2:4])
    grad_three = jnp.stack(pieces[4:6])

    one_parts = lamb_parts(w_one, m_one, v_one, grad_one)
    two_parts = lamb_parts(w_two, m_two, v_two, grad_two)
    three_parts = lamb_parts(w_three, m_three, v_three, grad_three)

    def squares(values):
        return jnp.concatenate([jnp.sum(v * v, axis=(1, 2)) for v in values])

    norms = jnp.sqrt(
        lax.psum(
            jnp.stack(
                [
                    squares([w_one, w_two, w_three]),
                    squares([one_parts[2], two_parts[2], three_parts[2]]),
                ]
            ),
            "mp",
        )
    )
    ratios = (norms[0] / norms[1])[:, None, None]
    one_new = w_one - 0.5 * ratios[0:2] * one_parts[2]
    two_new = w_two - 0.5 * ratios[2:4] * two_parts[2]
    three_new = w_three - 0.5 * ratios[4:6] * three_parts[2]
    table_new = jnp.stack([hidden_one, hidden_two], axis=0)
    return (
        loss_value,
        one_new,
        two_new,
        three_new,
        one_new.astype(BF16),
        two_new.astype(BF16),
        three_new.astype(BF16),
        one_parts[0],
        two_parts[0],
        three_parts[0],
        one_parts[1],
        two_parts[1],
        three_parts[1],
        norms,
        table_new,
    )


def solution(mesh):
    in_specs = (
        P("graph", None),
        P("graph", None),
        P("graph"),
        P("graph"),
        P("graph"),
        P("graph"),
        P(None, "mp", "graph"),
        P(None, None, "mp"),
        P(None, "mp", None),
        P(None, "mp", None),
        P(None, None, "mp"),
        P(None, None, "mp"),
        P(None, "mp", None),
        P(None, "mp", None),
        P(None, "mp", None),
        P(None, "mp", None),
    )
    out_specs = (
        P(),
        P(None, None, "mp"),
        P(None, "mp", None),
        P(None, "mp", None),
        P(None, None, "mp"),
        P(None, "mp", None),
        P(None, "mp", None),
        P(None, None, "mp"),
        P(None, "mp", None),
        P(None, "mp", None),
        P(None, None, "mp"),
        P(None, "mp", None),
        P(None, "mp", None),
        P(),
        P(None, "mp", "graph"),
    )
    return jax.shard_map(local, mesh=mesh, in_specs=in_specs, out_specs=out_specs, check_vma=False)
```

```python
import jax
import jax.numpy as jnp
from jax import lax
from jax.experimental import pallas as pl
from jax.experimental.pallas import tpu as pltpu
from jax.sharding import PartitionSpec as P

STEP = 3
F32 = jnp.float32
BF16 = jnp.bfloat16
DIGIT = 256
DIRECT_MOST = 8


def nt(left, right):
    return lax.dot_general(left, right, (((1,), (1,)), ((), ())), preferred_element_type=F32)


def nn(left, right):
    return lax.dot_general(left, right, (((1,), (0,)), ((), ())), preferred_element_type=F32)


def tn(left, right):
    return lax.dot_general(left, right, (((0,), (0,)), ((), ())), preferred_element_type=F32)


def kept(value):
    return lax.reduce_precision(value, 8, 7)


def in_two(value):
    high = kept(value)
    return high.astype(BF16), (value - high).astype(BF16)


def count_block(dst_rows, first, size):
    ids = lax.broadcasted_iota(jnp.int32, (size, dst_rows.shape[1]), 0) + first
    total = (ids == dst_rows[0:1]).astype(F32)
    for slot in range(1, dst_rows.shape[0]):
        total = total + (ids == dst_rows[slot : slot + 1]).astype(F32)
    return total.astype(BF16)


def pad_rows(value, rows):
    return jnp.pad(value, ((0, rows - value.shape[0]), (0, 0)))


def pad_lanes(value, lanes):
    return jnp.pad(value, ((0, 0), (0, lanes - value.shape[1])))


def lamb_parts(weights, first, second, grad):
    correction = 1.0 - 0.5**STEP
    first_new = 0.5 * first + 0.5 * grad
    second_new = 0.5 * second + 0.5 * grad * grad
    update = first_new / correction / (jnp.sqrt(second_new / correction) + 1e-06) + 0.01 * weights
    return (first_new, second_new, update)


def call(kernel, outs, *operands):
    space = pl.BlockSpec(memory_space=pltpu.VMEM)
    return pl.pallas_call(
        kernel,
        out_shape=[jax.ShapeDtypeStruct(shape, kind) for shape, kind in outs],
        in_specs=[space] * len(operands),
        out_specs=[space] * len(outs),
    )(*operands)


def over(row, value):
    return jnp.broadcast_to(row, value.shape)


def messages_kernel(features, edges, valid, table, one, two, three, first, own):
    in_units, nodes = features.shape
    fanout = edges.shape[0]
    units, hidden = two.shape[1:]
    wide_in = -(-in_units // 128) * 128
    classes = three.shape[0]
    rows = first.shape[0]
    dst = edges[...]
    high = dst // DIGIT
    tail = [high, dst - high * DIGIT, valid[...]]
    used = in_units + 2 * fanout + 1
    whole = jnp.concatenate(
        [features[...].astype(F32)]
        + [part.astype(F32) for part in tail]
        + [jnp.zeros((rows - used, nodes), F32)],
        axis=0,
    )
    first[...] = whole.astype(BF16)
    own[:, :nodes] = table[0].astype(BF16)
    at = nodes
    blank = jnp.zeros((units, wide_in - in_units), F32)
    for which in range(2):
        own[:, at : at + wide_in] = jnp.concatenate([one[which], blank], axis=1).astype(BF16)
        at += wide_in
    for which in range(2):
        own[:, at : at + hidden] = two[which].astype(BF16)
        at += hidden
    pair = jnp.concatenate([three[:, 0, :], three[:, 1, :]], axis=1)
    pair = jnp.concatenate([pair, jnp.zeros((units - classes, 2 * units), F32)], axis=0).T
    turned = jnp.concatenate([pair[:units], pair[units:]], axis=1)
    own[:, at : at + 2 * units] = turned.astype(BF16)


def back_kernel(edges, back):
    nodes = edges.shape[1]
    me = lax.axis_index("graph")
    for step in range(back.shape[0] // nodes):
        first = (me ^ step) * nodes
        back[step * nodes : (step + 1) * nodes, :] = count_block(edges, first, nodes)


def weights_kernel(*refs):
    count = len(refs) - 6
    blocks, (old, one, two_turned, three_turned, whole_two, whole_three) = (
        refs[:count],
        refs[count:],
    )
    units = blocks[0].shape[0]
    mine = lax.axis_index("mp")
    nodes = old.shape[1]
    span = one.shape[1]
    hidden = whole_two.shape[1] // 2
    for step, block in enumerate(blocks):
        place = pl.ds(pl.multiple_of((mine ^ step) * units, units), units)
        old[place, :] = block[:, :nodes]
        one[place, :] = block[:, nodes : nodes + span]
        whole_two[place, :] = block[:, nodes + span : nodes + span + 2 * hidden].astype(F32)
        whole_three[place, :] = block[:, nodes + span + 2 * hidden :].astype(F32)
    three_turned[...] = whole_three[...].T.astype(BF16)
    turned = whole_two[...].T
    whole_two_turned = turned.reshape(2, hidden, hidden)
    for which in range(2):
        part = whole_two_turned[which]
        picked = part[:units]
        for step in range(1, hidden // units):
            picked = jnp.where(mine == step, part[step * units : (step + 1) * units], picked)
        two_turned[:, which * hidden : (which + 1) * hidden] = picked.astype(BF16)


def one_kernel(in_units, fanout, *refs):
    count = len(refs) - 16
    blocks = refs[:count]
    (degree, fresh, table, old, one, two, two_turned) = refs[count : count + 7]
    (ahead, in_sums, gate, hidden_one, input_two, own_two, near_two, seeds, pre) = refs[count + 7 :]
    del two_turned
    nodes = degree.shape[1]
    rows = blocks[0].shape[0]
    units = own_two.shape[0]
    me = lax.axis_index("graph")
    mine = lax.axis_index("mp")
    wide = one.shape[1] // 2
    one_self, one_near = one[:, :rows], one[:, wide : wide + rows]
    base = in_units // 16 * 16
    totals = None
    sums = None
    seed_rows = None
    for step, block in enumerate(blocks):
        value = block[...]
        tail = block[base:, :].astype(F32)
        at = in_units - base
        digits = tail[at : at + fanout] * DIGIT + tail[at + fanout : at + 2 * fanout]
        seed_row = tail[at + 2 * fanout : at + 2 * fanout + 1]
        counts = count_block(digits.astype(jnp.int32), me * nodes, nodes)
        ahead[:, step * nodes : (step + 1) * nodes] = counts
        near = nn(one_near, value).astype(BF16)
        total, part = nt(near, counts), nt(value, counts)
        totals = total if totals is None else totals + total
        sums = part if sums is None else sums + part
        seed_rows = seed_row if seed_rows is None else seed_rows + seed_row
    in_sums[...] = sums
    seeds[...] = jnp.broadcast_to(jnp.sum(seed_rows, axis=1, keepdims=True), seeds.shape)
    degrees = degree[...].astype(F32)
    value = nn(one_self, blocks[0][...]) + totals / over(degrees, totals)
    pre[...] = value
    keep = over(fresh[...].astype(F32), value) > 0
    inputs = jnp.where(keep, jnp.maximum(value, 0.0), old[...].astype(F32)).astype(BF16)
    input_two[...] = inputs
    own = pre[pl.ds(pl.multiple_of(mine * units, units), units), :]
    keep = over(fresh[...].astype(F32), own) > 0
    hidden_one[...] = jnp.where(keep, jnp.maximum(own, 0.0), table[0])
    gate[...] = jnp.where(keep, jnp.where(own > 0, 1.0, 0.0), 0.0)
    own_two[...] = nn(two[0].astype(BF16), inputs)
    near_two[...] = nn(two[1].astype(BF16), inputs).astype(BF16)


def summed(blocks, counts, product):
    nodes = blocks[0].shape[1]
    total = None
    for step, block in enumerate(blocks):
        part = product(block[...], counts(step, nodes))
        total = part if total is None else total + part
    return total


def two_kernel(*refs):
    count = len(refs) - 9
    blocks = refs[:count]
    (ahead, own_two, degree, fresh, table, hidden_one) = refs[count : count + 6]
    (table_new, low_hidden, gate) = refs[count + 6 :]
    sums = summed(blocks, lambda s, n: ahead[:, s * n : (s + 1) * n], nt)
    value = own_two[...] + sums / over(degree[...].astype(F32), sums)
    keep = over(fresh[...].astype(F32), value) > 0
    hidden = jnp.where(keep, jnp.maximum(value, 0.0), table[1])
    table_new[0] = hidden_one[...]
    table_new[1] = hidden
    low_hidden[...] = hidden.astype(BF16)
    gate[...] = jnp.where(keep, jnp.where(value > 0, 1.0, 0.0), 0.0)


def three_kernel(*refs):
    count = len(refs) - 4
    blocks, (turned, own, near, whole) = refs[:count], refs[count:]
    units = blocks[0].shape[0]
    mine = lax.axis_index("mp")
    for step, block in enumerate(blocks):
        whole[pl.ds(pl.multiple_of((mine ^ step) * units, units), units), :] = block[...]
    both = nn(turned[...], whole[...])
    rows = own.shape[0]
    own[...] = both[:rows]
    near[...] = both[turned.shape[0] // 2 : turned.shape[0] // 2 + rows].astype(BF16)


def loss_kernel(classes, *refs):
    count = len(refs) - 8
    blocks = refs[:count]
    (ahead, own, degree, valid, labels, seeds) = refs[count : count + 6]
    (low_grad, message) = refs[count + 6 :]
    sums = summed(blocks, lambda s, n: ahead[:, s * n : (s + 1) * n], nt)
    degrees = over(degree[...].astype(F32), sums)
    logits = own[...] + sums / degrees
    row = lax.broadcasted_iota(jnp.int32, logits.shape, 0)
    real = row < classes
    logits = jnp.where(real, logits, -1e30)
    shifted = logits - over(jnp.max(logits, axis=0, keepdims=True), logits)
    scale = jnp.log(jnp.sum(jnp.exp(shifted), axis=0, keepdims=True))
    log_probs = jnp.where(real, shifted - over(scale, logits), 0.0)
    targets = jnp.where(row == over(labels[...], row), 1.0, 0.0)
    chosen = jnp.sum(targets * log_probs, axis=0, keepdims=True)
    per_seed = -(0.9 * chosen + 0.1 * (jnp.sum(log_probs, axis=0, keepdims=True) / classes))
    weight = valid[...].astype(F32)
    loss = jnp.sum(per_seed * weight, axis=1, keepdims=True)
    total = over(seeds[0:1, 0:1], logits)
    grad = over(weight, logits) * (jnp.exp(log_probs) - 0.9 * targets - 0.1 / classes) / total
    low = jnp.where(real, grad, 0.0).astype(BF16)
    low_grad[...] = low
    edge = low.astype(F32) / degrees
    lane = lax.broadcasted_iota(jnp.int32, logits.shape, 1)
    high = loss.astype(BF16).astype(F32)
    middle = (loss - high).astype(BF16).astype(F32)
    rest = loss - high - middle
    digits = jnp.where(
        lane == 0,
        over(high, logits),
        jnp.where(lane == 1, over(middle, logits), jnp.where(lane == 2, over(rest, logits), 0.0)),
    )
    message[...] = jnp.where(real, edge, jnp.where(row == classes, digits, 0.0)).astype(BF16)


def back_three_kernel(classes, *refs):
    count = len(refs) - 11
    blocks = refs[:count]
    (back, low_grad, low_hidden, own_message, gate, degree, seeds) = refs[count : count + 7]
    (loss, grads, low_two, edge_two) = refs[count + 7 :]
    rows = blocks[0].shape[0]
    units = low_hidden.shape[0]
    sums = summed(blocks, lambda s, n: back[s * n : (s + 1) * n, :], nn)
    near = sums.astype(BF16)
    base = classes // 16 * 16
    tail = None
    for block in blocks:
        part = block[base:, :].astype(F32)
        tail = part if tail is None else tail + part
    parts = jnp.sum(tail[classes - base : classes - base + 1, :128], axis=1, keepdims=True)
    loss[...] = over(parts, loss) / seeds[...]
    low = low_grad[...]
    at = own_message.shape[1] - 2 * units
    value = nn(own_message[:, at : at + rows], low)
    value = value + nn(own_message[:, at + units : at + units + rows], near)
    value = (value * gate[...]).astype(BF16)
    low_two[...] = value
    edge_two[...] = (value.astype(F32) / over(degree[...].astype(F32), gate)).astype(BF16)
    grads[...] = jnp.zeros(grads.shape, F32)
    grads[:rows, :units] = nt(low, low_hidden[...])
    grads[:rows, units:] = nt(near, low_hidden[...])


def back_two_kernel(*refs):
    count = len(refs) - 2
    blocks, (back, near) = refs[:count], refs[count:]
    near[...] = summed(blocks, lambda s, n: back[s * n : (s + 1) * n, :], nn).astype(BF16)


def back_one_kernel(peers, *refs):
    lows, nears = refs[:peers], refs[peers : 2 * peers]
    (two_turned, gate, degree, first, in_sums, input_two, grads_three) = refs[
        2 * peers : 2 * peers + 7
    ]
    (partial, whole_low, whole_near) = refs[2 * peers + 7 :]
    units = lows[0].shape[0]
    hidden = units * peers
    rows = first.shape[0]
    wide = -(-rows // 128) * 128
    mine = lax.axis_index("mp")
    for step in range(peers):
        place = pl.ds(pl.multiple_of((mine ^ step) * units, units), units)
        whole_low[place, :] = lows[step][...]
        whole_near[place, :] = nears[step][...]
    value = nn(two_turned[:, :hidden], whole_low[...])
    value = value + nn(two_turned[:, hidden:], whole_near[...])
    low = (value * gate[...]).astype(BF16)
    edge = (low.astype(F32) / over(degree[...].astype(F32), gate)).astype(BF16)
    sums = in_sums[...]
    high = sums.astype(BF16)
    rest = (sums - high.astype(F32)).astype(BF16)
    blank = jnp.zeros((units, wide - rows), F32)
    partial[:, :wide] = jnp.concatenate([nt(low, first[...]), blank], axis=1)
    partial[:, wide : 2 * wide] = jnp.concatenate([nt(edge, high) + nt(edge, rest), blank], axis=1)
    at = 2 * wide
    partial[:, at : at + hidden] = nt(lows[0][...], input_two[...])
    at += hidden
    partial[:, at : at + hidden] = nt(nears[0][...], input_two[...])
    at += hidden
    partial[:, at:] = grads_three[...]


def add_kernel(shares, out):
    total = shares[0]
    for step in range(1, shares.shape[0]):
        total = total + shares[step]
    for step in range(out.shape[0]):
        out[step] = total


def pieces_of(total, one, two, three):
    in_units, hidden = one.shape[2], two.shape[2]
    classes, units = three.shape[0], three.shape[2]
    wide = -(-in_units // 128) * 128
    at = 2 * wide + 2 * hidden
    return [
        (0, lambda ref: (ref, 0), total[:, :in_units]),
        (0, lambda ref: (ref, 1), total[:, wide : wide + in_units]),
        (1, lambda ref: (ref, 0), total[:, 2 * wide : 2 * wide + hidden]),
        (1, lambda ref: (ref, 1), total[:, 2 * wide + hidden : at]),
        (2, lambda ref: (ref, (slice(None), 0, slice(None))), total[:classes, at : at + units]),
        (2, lambda ref: (ref, (slice(None), 1, slice(None))), total[:classes, at + units :]),
    ]


def moments_kernel(total, *refs):
    weights, firsts, seconds = refs[0:3], refs[3:6], refs[6:9]
    firsts_new, seconds_new, updates = refs[9:12], refs[12:15], refs[15:18]
    squares = refs[18]
    row = lax.broadcasted_iota(jnp.int32, squares.shape, 0)
    lane = lax.broadcasted_iota(jnp.int32, squares.shape, 1)
    found = jnp.zeros(squares.shape, F32)
    for place, (which, at, grad) in enumerate(pieces_of(total[...], *weights)):
        index = at(None)[1]
        weight = weights[which][index]
        parts = lamb_parts(weight, firsts[which][index], seconds[which][index], grad)
        firsts_new[which][index] = parts[0]
        seconds_new[which][index] = parts[1]
        updates[which][index] = parts[2]
        for line, value in ((0, weight), (1, parts[2])):
            square = jnp.sum(value * value, axis=0, keepdims=True)
            square = jnp.sum(square, axis=1, keepdims=True)
            here = jnp.where(row == line, jnp.where(lane == place, 1.0, 0.0), 0.0)
            found = found + here * over(square, found)
    squares[...] = found


def steps_kernel(squares, *refs):
    weights, updates = refs[0:3], refs[3:6]
    news, copies, norms = refs[6:9], refs[9:12], refs[12]
    roots = jnp.sqrt(squares[...])
    norms[...] = roots
    for place in range(6):
        which = place // 2
        index = (slice(None), place % 2, slice(None)) if which == 2 else place % 2
        ratio = roots[0:1, place : place + 1] / roots[1:2, place : place + 1]
        weight = weights[which][index]
        new = weight - 0.5 * over(ratio, weight) * updates[which][index]
        news[which][index] = new
        copies[which][index] = new.astype(BF16)


def local_direct(
    features,
    edge_dst,
    degree,
    fresh,
    seed_mask,
    labels,
    table,
    w_one,
    w_two,
    w_three,
    m_one,
    v_one,
    m_two,
    v_two,
    m_three,
    v_three,
):
    devices = lax.axis_size("graph")
    peers = lax.axis_size("mp")
    nodes, in_units = features.shape
    fanout = edge_dst.shape[1]
    units = w_one.shape[2]
    hidden = w_two.shape[2]
    classes = w_three.shape[2]
    wide_in = -(-in_units // 128) * 128
    first_rows = -(-(in_units + 2 * fanout + 1) // 16) * 16
    class_rows = -(-(classes + 1) // 16) * 16
    line = (1, nodes)
    degree, fresh, valid, labels = [
        value.reshape(line) for value in (degree, fresh, seed_mask, labels)
    ]
    edges = edge_dst.T
    ones = [jnp.transpose(value, (0, 2, 1)) for value in (w_one, m_one, v_one)]
    twos = [w_two, m_two, v_two]
    threes = [jnp.transpose(value, (2, 0, 1)) for value in (w_three, m_three, v_three)]

    def exchange(block, axis, size):
        return [block] + [
            lax.ppermute(block, axis, [(i, i ^ step) for i in range(size)])
            for step in range(1, size)
        ]

    def gather(block):
        return exchange(block, "graph", devices)

    own_lanes = nodes + 2 * wide_in + 2 * hidden + 2 * units
    first, own = call(
        messages_kernel,
        [((first_rows, nodes), BF16), ((units, own_lanes), BF16)],
        features.T,
        edges,
        valid,
        table,
        ones[0],
        w_two,
        threes[0],
    )
    firsts = gather(first)
    owns = exchange(own, "mp", peers)
    (back,) = call(back_kernel, [((devices * nodes, nodes), BF16)], edges)
    old, one, two_turned, three_turned = pl.pallas_call(
        weights_kernel,
        out_shape=[
            jax.ShapeDtypeStruct((hidden, nodes), BF16),
            jax.ShapeDtypeStruct((hidden, 2 * wide_in), BF16),
            jax.ShapeDtypeStruct((units, 2 * hidden), BF16),
            jax.ShapeDtypeStruct((2 * units, hidden), BF16),
        ],
        scratch_shapes=[
            pltpu.VMEM((hidden, 2 * hidden), F32),
            pltpu.VMEM((hidden, 2 * units), F32),
        ],
    )(*owns)
    ahead, in_sums, gate_one, hidden_one, input_two, own_two, near_two, seeds = pl.pallas_call(
        lambda *refs: one_kernel(in_units, fanout, *refs),
        out_shape=[
            jax.ShapeDtypeStruct((nodes, devices * nodes), BF16),
            jax.ShapeDtypeStruct((first_rows, nodes), F32),
            jax.ShapeDtypeStruct((units, nodes), F32),
            jax.ShapeDtypeStruct((units, nodes), F32),
            jax.ShapeDtypeStruct((hidden, nodes), BF16),
            jax.ShapeDtypeStruct((units, nodes), F32),
            jax.ShapeDtypeStruct((units, nodes), BF16),
            jax.ShapeDtypeStruct((8, 128), F32),
        ],
        scratch_shapes=[pltpu.VMEM((hidden, nodes), F32)],
    )(*firsts, degree, fresh, table, old, one, w_two, two_turned)
    table_new, low_hidden, gate_two = call(
        two_kernel,
        [((2, units, nodes), F32), ((units, nodes), BF16), ((units, nodes), F32)],
        *gather(near_two),
        ahead,
        own_two,
        degree,
        fresh,
        table,
        hidden_one,
    )
    own_three, near_three = pl.pallas_call(
        three_kernel,
        out_shape=[
            jax.ShapeDtypeStruct((class_rows, nodes), F32),
            jax.ShapeDtypeStruct((class_rows, nodes), BF16),
        ],
        scratch_shapes=[pltpu.VMEM((hidden, nodes), BF16)],
    )(*exchange(low_hidden, "mp", peers), three_turned)
    low_three, message = call(
        lambda *refs: loss_kernel(classes, *refs),
        [((class_rows, nodes), BF16), ((class_rows, nodes), BF16)],
        *gather(near_three),
        ahead,
        own_three,
        degree,
        valid,
        labels,
        seeds,
    )
    loss, grads_three, low_two, edge_two = call(
        lambda *refs: back_three_kernel(classes, *refs),
        [
            ((8, 128), F32),
            ((units, 2 * units), F32),
            ((units, nodes), BF16),
            ((units, nodes), BF16),
        ],
        *gather(message),
        back,
        low_three,
        low_hidden,
        own,
        gate_two,
        degree,
        seeds,
    )
    edges_two = gather(edge_two)
    lows = exchange(low_two, "mp", peers)
    (near_grad,) = call(back_two_kernel, [((units, nodes), BF16)], *edges_two, back)
    nears = exchange(near_grad, "mp", peers)
    lanes = 2 * wide_in + 2 * hidden + 2 * units
    partial = pl.pallas_call(
        lambda *refs: back_one_kernel(peers, *refs),
        out_shape=jax.ShapeDtypeStruct((units, lanes), F32),
        scratch_shapes=[pltpu.VMEM((hidden, nodes), BF16), pltpu.VMEM((hidden, nodes), BF16)],
    )(*lows, *nears, two_turned, gate_one, degree, first, in_sums, input_two, grads_three)

    share = partial.reshape(devices, units // devices, lanes)
    share = lax.all_to_all(share, "graph", 0, 0)
    (share,) = call(add_kernel, [(share.shape, F32)], share)
    total = lax.all_to_all(share, "graph", 0, 0).reshape(units, lanes)
    shapes = [(value.shape, F32) for value in (ones[0], w_two, threes[0])]
    found = call(
        moments_kernel,
        shapes * 3 + [((8, 128), F32)],
        total,
        *(group[0] for group in (ones, twos, threes)),
        *(group[1] for group in (ones, twos, threes)),
        *(group[2] for group in (ones, twos, threes)),
    )
    found_norms = lax.psum(found[9], "mp")
    stepped = call(
        steps_kernel,
        shapes + [(shape, BF16) for shape, kind in shapes] + [((8, 128), F32)],
        found_norms,
        ones[0],
        w_two,
        threes[0],
        *found[6:9],
    )

    def restored(values):
        return (
            jnp.transpose(values[0], (0, 2, 1)),
            values[1],
            jnp.transpose(values[2], (1, 2, 0)),
        )

    return (
        loss[0, 0],
        *restored(stepped[0:3]),
        *restored(stepped[3:6]),
        *restored(found[0:3]),
        *restored(found[3:6]),
        stepped[6][:2, :6],
        table_new,
    )


def local_wide(
    features,
    edge_dst,
    degree,
    fresh,
    seed_mask,
    labels,
    table,
    w_one,
    w_two,
    w_three,
    m_one,
    v_one,
    m_two,
    v_two,
    m_three,
    v_three,
):
    devices = lax.axis_size("graph")
    me = lax.axis_index("graph")
    mine = lax.axis_index("mp")
    nodes, in_units = features.shape
    fanout = edge_dst.shape[1]
    units = w_one.shape[2]
    hidden = w_two.shape[2]
    classes = w_three.shape[2]
    degrees = degree.astype(F32)[None, :]
    is_fresh = (fresh > 0)[None, :]
    valid = seed_mask.astype(F32)[None, :]

    def gather(block):
        return lax.all_gather(block, "graph", axis=1, tiled=True)

    dst_rows = edge_dst.T
    feature_rows = features.T
    first_rows = in_units + 2 * fanout + 1
    first_message = pad_rows(
        jnp.concatenate(
            [
                feature_rows,
                (dst_rows // DIGIT).astype(BF16),
                (dst_rows % DIGIT).astype(BF16),
                valid.astype(BF16),
            ],
            axis=0,
        ),
        -(-first_rows // 16) * 16,
    )
    firsts = gather(first_message)
    low_one = jnp.transpose(w_one.astype(BF16), (0, 2, 1))
    low_two = w_two.astype(BF16)
    low_three = w_three.astype(BF16)
    wide_in = -(-in_units // 128) * 128
    wide_class = -(-classes // 64) * 64
    own_message = jnp.concatenate(
        [
            table[0].astype(BF16),
            pad_lanes(low_one[0], wide_in),
            pad_lanes(low_one[1], wide_in),
            low_two[0],
            low_two[1],
            pad_lanes(low_three[0], wide_class),
            pad_lanes(low_three[1], wide_class),
        ],
        axis=1,
    )
    whole = lax.all_gather(own_message, "mp", axis=0, tiled=True)
    cuts = [nodes, wide_in, wide_in, hidden, hidden, wide_class, wide_class]
    pieces = []
    at = 0
    for cut in cuts:
        pieces.append(whole[:, at : at + cut])
        at += cut
    old_one, all_one_self, all_one_near = pieces[0], pieces[1][:, :in_units], pieces[2][:, :in_units]
    all_two_self, all_two_near = pieces[3], pieces[4]
    all_three_self, all_three_near = pieces[5][:, :classes], pieces[6][:, :classes]

    all_features = firsts[:in_units]
    high = firsts[in_units : in_units + fanout].astype(F32)
    low = firsts[in_units + fanout : in_units + 2 * fanout].astype(F32)
    all_dst = (high * DIGIT + low).astype(jnp.int32)
    seed_count = jnp.sum(firsts[in_units + 2 * fanout].astype(F32))

    def spread(all_rows):
        def step(total, block):
            rows = lax.dynamic_slice_in_dim(all_rows, block * nodes, nodes, 1)
            dst = lax.dynamic_slice_in_dim(all_dst, block * nodes, nodes, 1)
            return total + nt(rows, count_block(dst, me * nodes, nodes)), None

        start = jnp.zeros((all_rows.shape[0], nodes), F32)
        return lax.scan(step, start, jnp.arange(devices, dtype=jnp.int32))[0]

    def collect(all_rows):
        def step(total, block):
            rows = lax.dynamic_slice_in_dim(all_rows, block * nodes, nodes, 1)
            return total + nn(rows, count_block(dst_rows, block * nodes, nodes)), None

        start = jnp.zeros((all_rows.shape[0], nodes), F32)
        return lax.scan(step, start, jnp.arange(devices, dtype=jnp.int32))[0]

    def mine_of(rows):
        return lax.dynamic_slice_in_dim(rows, mine * units, units, 0)

    near_one = nn(all_one_near, all_features).astype(BF16)
    in_sums = spread(all_features)
    pre_one = nn(all_one_self, feature_rows) + spread(near_one) / degrees
    input_two = jnp.where(is_fresh, jax.nn.relu(pre_one).astype(BF16), old_one)
    pre_one = mine_of(pre_one)
    hidden_one = jnp.where(is_fresh, jax.nn.relu(pre_one), table[0])
    near_two = nn(low_two[1], input_two).astype(BF16)
    pre_two = nn(low_two[0], input_two) + spread(gather(near_two)) / degrees
    hidden_two = jnp.where(is_fresh, jax.nn.relu(pre_two), table[1])
    low_hidden = hidden_two.astype(BF16)
    input_three = lax.all_gather(low_hidden, "mp", axis=0, tiled=True)
    near_three = tn(all_three_near, input_three).astype(BF16)
    class_rows = -(-(classes + 1) // 16) * 16
    sums = spread(gather(pad_rows(near_three, class_rows)))[:classes]
    logits = tn(all_three_self, input_three) + sums / degrees
    log_probs = jax.nn.log_softmax(logits, axis=0)
    targets = (lax.broadcasted_iota(jnp.int32, logits.shape, 0) == labels[None, :]).astype(F32)
    per_seed = -(
        0.9 * jnp.sum(targets * log_probs, axis=0, keepdims=True)
        + 0.1 * jnp.mean(log_probs, axis=0, keepdims=True)
    )
    loss_part = jnp.sum(per_seed * valid)

    grad_logits = valid * (jnp.exp(log_probs) - 0.9 * targets - 0.1 / classes) / seed_count
    low_grad_three = grad_logits.astype(BF16)
    edge_three = (low_grad_three.astype(F32) / degrees).astype(BF16)
    lanes = lax.broadcasted_iota(jnp.int32, (1, nodes), 1)
    loss_high = kept(loss_part)
    loss_mid = kept(loss_part - loss_high)
    loss_row = jnp.where(
        lanes == 0,
        loss_high,
        jnp.where(
            lanes == 1, loss_mid, jnp.where(lanes == 2, loss_part - loss_high - loss_mid, 0.0)
        ),
    ).astype(BF16)
    thirds = gather(pad_rows(jnp.concatenate([edge_three, loss_row], axis=0), class_rows))
    loss_value = jnp.sum(thirds[classes].astype(F32)) / seed_count
    near_grad_three = collect(thirds)[:classes].astype(BF16)
    grads_three = [nt(low_hidden, low_grad_three), nt(low_hidden, near_grad_three)]
    grad_hidden_two = nn(low_three[0], low_grad_three) + nn(low_three[1], near_grad_three)
    low_grad_two = jnp.where(is_fresh & (pre_two > 0), grad_hidden_two, 0.0).astype(BF16)
    edge_two = (low_grad_two.astype(F32) / degrees).astype(BF16)
    near_grad_two = collect(gather(edge_two)).astype(BF16)
    grads_two = [nt(low_grad_two, input_two), nt(near_grad_two, input_two)]
    both = lax.all_gather(
        jnp.concatenate([low_grad_two, near_grad_two], axis=1), "mp", axis=0, tiled=True
    )
    columns_self = lax.dynamic_slice_in_dim(all_two_self, mine * units, units, 1)
    columns_near = lax.dynamic_slice_in_dim(all_two_near, mine * units, units, 1)
    grad_hidden_one = tn(columns_self, both[:, :nodes]) + tn(columns_near, both[:, nodes:])
    low_grad_one = jnp.where(is_fresh & (pre_one > 0), grad_hidden_one, 0.0).astype(BF16)
    edge_one = (low_grad_one.astype(F32) / degrees).astype(BF16)
    sums_high, sums_low = in_two(in_sums)
    grads_one = [
        nt(low_grad_one, feature_rows),
        nt(edge_one, sums_high) + nt(edge_one, sums_low),
    ]

    partial = jnp.concatenate(
        [pad_lanes(g, wide_in) for g in grads_one]
        + grads_two
        + [pad_lanes(g, wide_class) for g in grads_three],
        axis=1,
    )
    share = partial.reshape(devices, units // devices, partial.shape[1])
    share = jnp.sum(lax.all_to_all(share, "graph", 0, 0), axis=0)
    share = jnp.broadcast_to(share[None], (devices,) + share.shape)
    total = lax.all_to_all(share, "graph", 0, 0).reshape(partial.shape)
    at = 0
    pieces = []
    for cut, use in (
        (wide_in, in_units),
        (wide_in, in_units),
        (hidden, hidden),
        (hidden, hidden),
        (wide_class, classes),
        (wide_class, classes),
    ):
        pieces.append(total[:, at : at + use])
        at += cut
    grad_one = jnp.stack([pieces[0].T, pieces[1].T])
    grad_two = jnp.stack(pieces[2:4])
    grad_three = jnp.stack(pieces[4:6])

    one_parts = lamb_parts(w_one, m_one, v_one, grad_one)
    two_parts = lamb_parts(w_two, m_two, v_two, grad_two)
    three_parts = lamb_parts(w_three, m_three, v_three, grad_three)

    def squares(values):
        return jnp.concatenate([jnp.sum(v * v, axis=(1, 2)) for v in values])

    norms = jnp.sqrt(
        lax.psum(
            jnp.stack(
                [
                    squares([w_one, w_two, w_three]),
                    squares([one_parts[2], two_parts[2], three_parts[2]]),
                ]
            ),
            "mp",
        )
    )
    ratios = (norms[0] / norms[1])[:, None, None]
    one_new = w_one - 0.5 * ratios[0:2] * one_parts[2]
    two_new = w_two - 0.5 * ratios[2:4] * two_parts[2]
    three_new = w_three - 0.5 * ratios[4:6] * three_parts[2]
    table_new = jnp.stack([hidden_one, hidden_two], axis=0)
    return (
        loss_value,
        one_new,
        two_new,
        three_new,
        one_new.astype(BF16),
        two_new.astype(BF16),
        three_new.astype(BF16),
        one_parts[0],
        two_parts[0],
        three_parts[0],
        one_parts[1],
        two_parts[1],
        three_parts[1],
        norms,
        table_new,
    )


def solution(mesh):
    in_specs = (
        P("graph", None),
        P("graph", None),
        P("graph"),
        P("graph"),
        P("graph"),
        P("graph"),
        P(None, "mp", "graph"),
        P(None, None, "mp"),
        P(None, "mp", None),
        P(None, "mp", None),
        P(None, None, "mp"),
        P(None, None, "mp"),
        P(None, "mp", None),
        P(None, "mp", None),
        P(None, "mp", None),
        P(None, "mp", None),
    )
    out_specs = (
        P(),
        P(None, None, "mp"),
        P(None, "mp", None),
        P(None, "mp", None),
        P(None, None, "mp"),
        P(None, "mp", None),
        P(None, "mp", None),
        P(None, None, "mp"),
        P(None, "mp", None),
        P(None, "mp", None),
        P(None, None, "mp"),
        P(None, "mp", None),
        P(None, "mp", None),
        P(),
        P(None, "mp", "graph"),
    )
    axes = mesh.shape["graph"], mesh.shape["mp"]
    few = axes[0] <= DIRECT_MOST and all(size & (size - 1) == 0 for size in axes)
    local = local_direct if few else local_wide
    return jax.shard_map(local, mesh=mesh, in_specs=in_specs, out_specs=out_specs, check_vma=False)
```

```python
import jax
import jax.numpy as jnp
from jax import lax
from jax.experimental import pallas as pl
from jax.experimental.pallas import tpu as pltpu
from jax.sharding import PartitionSpec as P

STEP = 3
F32 = jnp.float32
BF16 = jnp.bfloat16
DIGIT = 256
DIRECT_MOST = 8


def nt(left, right):
    return lax.dot_general(left, right, (((1,), (1,)), ((), ())), preferred_element_type=F32)


def nn(left, right):
    return lax.dot_general(left, right, (((1,), (0,)), ((), ())), preferred_element_type=F32)


def tn(left, right):
    return lax.dot_general(left, right, (((0,), (0,)), ((), ())), preferred_element_type=F32)


def kept(value):
    return lax.reduce_precision(value, 8, 7)


def in_two(value):
    high = kept(value)
    return high.astype(BF16), (value - high).astype(BF16)


def count_block(dst_rows, first, size):
    ids = lax.broadcasted_iota(jnp.int32, (size, dst_rows.shape[1]), 0) + first
    total = (ids == dst_rows[0:1]).astype(F32)
    for slot in range(1, dst_rows.shape[0]):
        total = total + (ids == dst_rows[slot : slot + 1]).astype(F32)
    return total.astype(BF16)


def pad_rows(value, rows):
    return jnp.pad(value, ((0, rows - value.shape[0]), (0, 0)))


def pad_lanes(value, lanes):
    return jnp.pad(value, ((0, 0), (0, lanes - value.shape[1])))


def lamb_parts(weights, first, second, grad):
    correction = 1.0 - 0.5**STEP
    first_new = 0.5 * first + 0.5 * grad
    second_new = 0.5 * second + 0.5 * grad * grad
    update = first_new / correction / (jnp.sqrt(second_new / correction) + 1e-06) + 0.01 * weights
    return (first_new, second_new, update)


VMEM_BYTES = 24 * 2**20


def call(kernel, outs, *operands, scratch=()):
    space = pl.BlockSpec(memory_space=pltpu.VMEM)
    found = pl.pallas_call(
        kernel,
        out_shape=[
            jax.ShapeDtypeStruct(*out[:2]) if len(out) > 2 else pltpu.VMEM(*out) for out in outs
        ],
        in_specs=[space] * len(operands),
        out_specs=[space] * len(outs),
        scratch_shapes=[pltpu.VMEM(*each) for each in scratch],
        compiler_params=pltpu.CompilerParams(vmem_limit_bytes=VMEM_BYTES),
    )(*(pltpu.with_memory_space_constraint(value, pltpu.VMEM) for value in operands))
    return found


def over(row, value):
    return jnp.broadcast_to(row, value.shape)


def messages_kernel(features, edges, valid, table, one, two, three, first, own):
    in_units, nodes = features.shape
    fanout = edges.shape[0]
    units, hidden = two.shape[1:]
    wide_in = -(-in_units // 128) * 128
    classes = three.shape[0]
    rows = first.shape[0]
    dst = edges[...]
    high = dst // DIGIT
    tail = [high, dst - high * DIGIT, valid[...]]
    used = in_units + 2 * fanout + 1
    whole = jnp.concatenate(
        [features[...].astype(F32)]
        + [part.astype(F32) for part in tail]
        + [jnp.zeros((rows - used, nodes), F32)],
        axis=0,
    )
    first[...] = whole.astype(BF16)
    own[:, :nodes] = table[0].astype(BF16)
    at = nodes
    blank = jnp.zeros((units, wide_in - in_units), F32)
    for which in range(2):
        own[:, at : at + wide_in] = jnp.concatenate([one[which], blank], axis=1).astype(BF16)
        at += wide_in
    for which in range(2):
        own[:, at : at + hidden] = two[which].astype(BF16)
        at += hidden
    pair = jnp.concatenate([three[:, 0, :], three[:, 1, :]], axis=1)
    pair = jnp.concatenate([pair, jnp.zeros((units - classes, 2 * units), F32)], axis=0).T
    turned = jnp.concatenate([pair[:units], pair[units:]], axis=1)
    own[:, at : at + 2 * units] = turned.astype(BF16)


def weights_kernel(*refs):
    count = len(refs) - 8
    blocks = refs[:count]
    (edges, old, one, two_turned, three_turned, back, whole_two, whole_three) = refs[count:]
    units = blocks[0].shape[0]
    mine = lax.axis_index("mp")
    nodes = old.shape[1]
    span = one.shape[1]
    hidden = whole_two.shape[1] // 2
    for step, block in enumerate(blocks):
        place = pl.ds(pl.multiple_of((mine ^ step) * units, units), units)
        old[place, :] = block[:, :nodes]
        one[place, :] = block[:, nodes : nodes + span]
        whole_two[place, :] = block[:, nodes + span : nodes + span + 2 * hidden].astype(F32)
        whole_three[place, :] = block[:, nodes + span + 2 * hidden :].astype(F32)
    three_turned[...] = whole_three[...].T.astype(BF16)
    turned = whole_two[...].T
    whole_two_turned = turned.reshape(2, hidden, hidden)
    for which in range(2):
        part = whole_two_turned[which]
        picked = part[:units]
        for step in range(1, hidden // units):
            picked = jnp.where(mine == step, part[step * units : (step + 1) * units], picked)
        two_turned[:, which * hidden : (which + 1) * hidden] = picked.astype(BF16)
    me = lax.axis_index("graph")
    for step in range(back.shape[0] // nodes):
        counts = count_block(edges, (me ^ step) * nodes, nodes)
        back[step * nodes : (step + 1) * nodes, :] = counts


def one_kernel(in_units, fanout, *refs):
    count = len(refs) - 15
    blocks = refs[:count]
    (degree, fresh, table, old, one, two) = refs[count : count + 6]
    (ahead, in_sums, gate, hidden_one, input_two, own_two, near_two, seeds, pre) = refs[count + 6 :]
    nodes = degree.shape[1]
    rows = blocks[0].shape[0]
    units = own_two.shape[0]
    me = lax.axis_index("graph")
    mine = lax.axis_index("mp")
    wide = one.shape[1] // 2
    one_self, one_near = one[:, :rows], one[:, wide : wide + rows]
    base = in_units // 16 * 16
    totals = None
    sums = None
    seed_rows = None
    for step, block in enumerate(blocks):
        value = block[...]
        tail = block[base:, :].astype(F32)
        at = in_units - base
        digits = tail[at : at + fanout] * DIGIT + tail[at + fanout : at + 2 * fanout]
        seed_row = tail[at + 2 * fanout : at + 2 * fanout + 1]
        counts = count_block(digits.astype(jnp.int32), me * nodes, nodes)
        ahead[:, step * nodes : (step + 1) * nodes] = counts
        near = nn(one_near, value).astype(BF16)
        total, part = nt(near, counts), nt(value, counts)
        totals = total if totals is None else totals + total
        sums = part if sums is None else sums + part
        seed_rows = seed_row if seed_rows is None else seed_rows + seed_row
    in_sums[...] = sums
    seeds[...] = jnp.broadcast_to(jnp.sum(seed_rows, axis=1, keepdims=True), seeds.shape)
    degrees = degree[...].astype(F32)
    value = nn(one_self, blocks[0][...]) + totals / over(degrees, totals)
    pre[...] = value
    keep = over(fresh[...].astype(F32), value) > 0
    inputs = jnp.where(keep, jnp.maximum(value, 0.0), old[...].astype(F32)).astype(BF16)
    input_two[...] = inputs
    own = pre[pl.ds(pl.multiple_of(mine * units, units), units), :]
    keep = over(fresh[...].astype(F32), own) > 0
    hidden_one[...] = jnp.where(keep, jnp.maximum(own, 0.0), table[0])
    gate[...] = jnp.where(keep, jnp.where(own > 0, 1.0, 0.0), 0.0)
    own_two[...] = nn(two[0].astype(BF16), inputs)
    near_two[...] = nn(two[1].astype(BF16), inputs).astype(BF16)


def summed(blocks, counts, product):
    nodes = blocks[0].shape[1]
    total = None
    for step, block in enumerate(blocks):
        part = product(block[...], counts(step, nodes))
        total = part if total is None else total + part
    return total


def two_kernel(*refs):
    count = len(refs) - 9
    blocks = refs[:count]
    (ahead, own_two, degree, fresh, table, hidden_one) = refs[count : count + 6]
    (table_new, low_hidden, gate) = refs[count + 6 :]
    sums = summed(blocks, lambda s, n: ahead[:, s * n : (s + 1) * n], nt)
    value = own_two[...] + sums / over(degree[...].astype(F32), sums)
    keep = over(fresh[...].astype(F32), value) > 0
    hidden = jnp.where(keep, jnp.maximum(value, 0.0), table[1])
    table_new[0] = hidden_one[...]
    table_new[1] = hidden
    low_hidden[...] = hidden.astype(BF16)
    gate[...] = jnp.where(keep, jnp.where(value > 0, 1.0, 0.0), 0.0)


def three_kernel(*refs):
    count = len(refs) - 4
    blocks, (turned, own, near, whole) = refs[:count], refs[count:]
    units = blocks[0].shape[0]
    mine = lax.axis_index("mp")
    for step, block in enumerate(blocks):
        whole[pl.ds(pl.multiple_of((mine ^ step) * units, units), units), :] = block[...]
    both = nn(turned[...], whole[...])
    rows = own.shape[0]
    own[...] = both[:rows]
    near[...] = both[turned.shape[0] // 2 : turned.shape[0] // 2 + rows].astype(BF16)


def loss_kernel(classes, *refs):
    count = len(refs) - 8
    blocks = refs[:count]
    (ahead, own, degree, valid, labels, seeds) = refs[count : count + 6]
    (low_grad, message) = refs[count + 6 :]
    sums = summed(blocks, lambda s, n: ahead[:, s * n : (s + 1) * n], nt)
    degrees = over(degree[...].astype(F32), sums)
    logits = own[...] + sums / degrees
    row = lax.broadcasted_iota(jnp.int32, logits.shape, 0)
    real = row < classes
    logits = jnp.where(real, logits, -1e30)
    shifted = logits - over(jnp.max(logits, axis=0, keepdims=True), logits)
    scale = jnp.log(jnp.sum(jnp.exp(shifted), axis=0, keepdims=True))
    log_probs = jnp.where(real, shifted - over(scale, logits), 0.0)
    targets = jnp.where(row == over(labels[...], row), 1.0, 0.0)
    chosen = jnp.sum(targets * log_probs, axis=0, keepdims=True)
    per_seed = -(0.9 * chosen + 0.1 * (jnp.sum(log_probs, axis=0, keepdims=True) / classes))
    weight = valid[...].astype(F32)
    loss = jnp.sum(per_seed * weight, axis=1, keepdims=True)
    total = over(seeds[0:1, 0:1], logits)
    grad = over(weight, logits) * (jnp.exp(log_probs) - 0.9 * targets - 0.1 / classes) / total
    low = jnp.where(real, grad, 0.0).astype(BF16)
    low_grad[...] = low
    edge = low.astype(F32) / degrees
    lane = lax.broadcasted_iota(jnp.int32, logits.shape, 1)
    high = loss.astype(BF16).astype(F32)
    middle = (loss - high).astype(BF16).astype(F32)
    rest = loss - high - middle
    digits = jnp.where(
        lane == 0,
        over(high, logits),
        jnp.where(lane == 1, over(middle, logits), jnp.where(lane == 2, over(rest, logits), 0.0)),
    )
    message[...] = jnp.where(real, edge, jnp.where(row == classes, digits, 0.0)).astype(BF16)


def back_three_kernel(classes, *refs):
    count = len(refs) - 11
    blocks = refs[:count]
    (back, low_grad, low_hidden, own_message, gate, degree, seeds) = refs[count : count + 7]
    (loss, grads, low_two, edge_two) = refs[count + 7 :]
    rows = blocks[0].shape[0]
    units = low_hidden.shape[0]
    sums = summed(blocks, lambda s, n: back[s * n : (s + 1) * n, :], nn)
    near = sums.astype(BF16)
    base = classes // 16 * 16
    tail = None
    for block in blocks:
        part = block[base:, :].astype(F32)
        tail = part if tail is None else tail + part
    parts = jnp.sum(tail[classes - base : classes - base + 1, :128], axis=1, keepdims=True)
    loss[...] = parts / seeds[0:1, 0:1]
    low = low_grad[...]
    at = own_message.shape[1] - 2 * units
    value = nn(own_message[:, at : at + rows], low)
    value = value + nn(own_message[:, at + units : at + units + rows], near)
    value = (value * gate[...]).astype(BF16)
    low_two[...] = value
    edge_two[...] = (value.astype(F32) / over(degree[...].astype(F32), gate)).astype(BF16)
    grads[...] = jnp.zeros(grads.shape, F32)
    grads[:rows, :units] = nt(low, low_hidden[...])
    grads[:rows, units:] = nt(near, low_hidden[...])


def back_two_kernel(*refs):
    count = len(refs) - 2
    blocks, (back, near) = refs[:count], refs[count:]
    near[...] = summed(blocks, lambda s, n: back[s * n : (s + 1) * n, :], nn).astype(BF16)


def back_one_kernel(peers, *refs):
    lows, nears = refs[:peers], refs[peers : 2 * peers]
    (two_turned, gate, degree, first, in_sums, input_two, grads_three) = refs[
        2 * peers : 2 * peers + 7
    ]
    (partial, whole_low, whole_near) = refs[2 * peers + 7 :]
    units = lows[0].shape[0]
    hidden = units * peers
    rows = first.shape[0]
    wide = -(-rows // 128) * 128
    mine = lax.axis_index("mp")
    for step in range(peers):
        place = pl.ds(pl.multiple_of((mine ^ step) * units, units), units)
        whole_low[place, :] = lows[step][...]
        whole_near[place, :] = nears[step][...]
    value = nn(two_turned[:, :hidden], whole_low[...])
    value = value + nn(two_turned[:, hidden:], whole_near[...])
    low = (value * gate[...]).astype(BF16)
    edge = (low.astype(F32) / over(degree[...].astype(F32), gate)).astype(BF16)
    sums = in_sums[...]
    high = sums.astype(BF16)
    rest = (sums - high.astype(F32)).astype(BF16)
    blank = jnp.zeros((units, wide - rows), F32)
    partial[:, :wide] = jnp.concatenate([nt(low, first[...]), blank], axis=1)
    partial[:, wide : 2 * wide] = jnp.concatenate([nt(edge, high) + nt(edge, rest), blank], axis=1)
    at = 2 * wide
    partial[:, at : at + hidden] = nt(lows[0][...], input_two[...])
    at += hidden
    partial[:, at : at + hidden] = nt(nears[0][...], input_two[...])
    at += hidden
    partial[:, at:] = grads_three[...]


def add_kernel(shares, out):
    total = shares[0]
    for step in range(1, shares.shape[0]):
        total = total + shares[step]
    for step in range(out.shape[0]):
        out[step] = total


def pieces_of(total, one, two, three):
    in_units, hidden = one.shape[2], two.shape[2]
    classes, units = three.shape[0], three.shape[2]
    wide = -(-in_units // 128) * 128
    at = 2 * wide + 2 * hidden
    return [
        (0, lambda ref: (ref, 0), total[:, :in_units]),
        (0, lambda ref: (ref, 1), total[:, wide : wide + in_units]),
        (1, lambda ref: (ref, 0), total[:, 2 * wide : 2 * wide + hidden]),
        (1, lambda ref: (ref, 1), total[:, 2 * wide + hidden : at]),
        (2, lambda ref: (ref, (slice(None), 0, slice(None))), total[:classes, at : at + units]),
        (2, lambda ref: (ref, (slice(None), 1, slice(None))), total[:classes, at + units :]),
    ]


def moments_kernel(total, *refs):
    weights, firsts, seconds = refs[0:3], refs[3:6], refs[6:9]
    firsts_new, seconds_new, updates = refs[9:12], refs[12:15], refs[15:18]
    squares = refs[18]
    row = lax.broadcasted_iota(jnp.int32, squares.shape, 0)
    lane = lax.broadcasted_iota(jnp.int32, squares.shape, 1)
    found = jnp.zeros(squares.shape, F32)
    for place, (which, at, grad) in enumerate(pieces_of(total[...], *weights)):
        index = at(None)[1]
        weight = weights[which][index]
        parts = lamb_parts(weight, firsts[which][index], seconds[which][index], grad)
        firsts_new[which][index] = parts[0]
        seconds_new[which][index] = parts[1]
        updates[which][index] = parts[2]
        for line, value in ((0, weight), (1, parts[2])):
            square = jnp.sum(value * value, axis=0, keepdims=True)
            square = jnp.sum(square, axis=1, keepdims=True)
            here = jnp.where(row == line, jnp.where(lane == place, 1.0, 0.0), 0.0)
            found = found + here * over(square, found)
    squares[...] = found


def steps_kernel(squares, *refs):
    weights, updates = refs[0:3], refs[3:6]
    news, copies, norms = refs[6:9], refs[9:12], refs[12]
    roots = jnp.sqrt(squares[...])
    norms[...] = roots
    for place in range(6):
        which = place // 2
        index = (slice(None), place % 2, slice(None)) if which == 2 else place % 2
        ratio = roots[0:1, place : place + 1] / roots[1:2, place : place + 1]
        weight = weights[which][index]
        new = weight - 0.5 * over(ratio, weight) * updates[which][index]
        news[which][index] = new
        copies[which][index] = new.astype(BF16)


def local_direct(
    features,
    edge_dst,
    degree,
    fresh,
    seed_mask,
    labels,
    table,
    w_one,
    w_two,
    w_three,
    m_one,
    v_one,
    m_two,
    v_two,
    m_three,
    v_three,
):
    devices = lax.axis_size("graph")
    peers = lax.axis_size("mp")
    nodes, in_units = features.shape
    fanout = edge_dst.shape[1]
    units = w_one.shape[2]
    hidden = w_two.shape[2]
    classes = w_three.shape[2]
    wide_in = -(-in_units // 128) * 128
    first_rows = -(-(in_units + 2 * fanout + 1) // 16) * 16
    class_rows = -(-(classes + 1) // 16) * 16
    line = (1, nodes)
    degree, fresh, valid, labels = [
        value.reshape(line) for value in (degree, fresh, seed_mask, labels)
    ]
    edges = edge_dst.T
    ones = [jnp.transpose(value, (0, 2, 1)) for value in (w_one, m_one, v_one)]
    twos = [w_two, m_two, v_two]
    threes = [jnp.transpose(value, (2, 0, 1)) for value in (w_three, m_three, v_three)]

    def exchange(block, axis, size):
        return [block] + [
            lax.ppermute(block, axis, [(i, i ^ step) for i in range(size)])
            for step in range(1, size)
        ]

    def gather(block):
        return exchange(block, "graph", devices)

    own_lanes = nodes + 2 * wide_in + 2 * hidden + 2 * units
    first, own = call(
        messages_kernel,
        [((first_rows, nodes), BF16), ((units, own_lanes), BF16)],
        features.T,
        edges,
        valid,
        table,
        ones[0],
        w_two,
        threes[0],
    )
    firsts = gather(first)
    owns = exchange(own, "mp", peers)
    old, one, two_turned, three_turned, back = call(
        weights_kernel,
        [
            ((hidden, nodes), BF16),
            ((hidden, 2 * wide_in), BF16),
            ((units, 2 * hidden), BF16),
            ((2 * units, hidden), BF16),
            ((devices * nodes, nodes), BF16),
        ],
        *owns,
        edges,
        scratch=[((hidden, 2 * hidden), F32), ((hidden, 2 * units), F32)],
    )
    ahead, in_sums, gate_one, hidden_one, input_two, own_two, near_two, seeds = call(
        lambda *refs: one_kernel(in_units, fanout, *refs),
        [
            ((nodes, devices * nodes), BF16),
            ((first_rows, nodes), F32),
            ((units, nodes), F32),
            ((units, nodes), F32),
            ((hidden, nodes), BF16),
            ((units, nodes), F32),
            ((units, nodes), BF16),
            ((8, 128), F32),
        ],
        *firsts,
        degree,
        fresh,
        table,
        old,
        one,
        w_two,
        scratch=[((hidden, nodes), F32)],
    )
    table_new, low_hidden, gate_two = call(
        two_kernel,
        [((2, units, nodes), F32), ((units, nodes), BF16), ((units, nodes), F32)],
        *gather(near_two),
        ahead,
        own_two,
        degree,
        fresh,
        table,
        hidden_one,
    )
    own_three, near_three = call(
        three_kernel,
        [((class_rows, nodes), F32), ((class_rows, nodes), BF16)],
        *exchange(low_hidden, "mp", peers),
        three_turned,
        scratch=[((hidden, nodes), BF16)],
    )
    low_three, message = call(
        lambda *refs: loss_kernel(classes, *refs),
        [((class_rows, nodes), BF16), ((class_rows, nodes), BF16)],
        *gather(near_three),
        ahead,
        own_three,
        degree,
        valid,
        labels,
        seeds,
    )
    loss, grads_three, low_two, edge_two = call(
        lambda *refs: back_three_kernel(classes, *refs),
        [
            ((1, 1), F32, 0),
            ((units, 2 * units), F32),
            ((units, nodes), BF16),
            ((units, nodes), BF16),
        ],
        *gather(message),
        back,
        low_three,
        low_hidden,
        own,
        gate_two,
        degree,
        seeds,
    )
    edges_two = gather(edge_two)
    lows = exchange(low_two, "mp", peers)
    (near_grad,) = call(back_two_kernel, [((units, nodes), BF16)], *edges_two, back)
    nears = exchange(near_grad, "mp", peers)
    lanes = 2 * wide_in + 2 * hidden + 2 * units
    (partial,) = call(
        lambda *refs: back_one_kernel(peers, *refs),
        [((units, lanes), F32)],
        *lows,
        *nears,
        two_turned,
        gate_one,
        degree,
        first,
        in_sums,
        input_two,
        grads_three,
        scratch=[((hidden, nodes), BF16)] * 2,
    )

    share = partial.reshape(devices, units // devices, lanes)
    share = lax.all_to_all(share, "graph", 0, 0)
    (share,) = call(add_kernel, [(share.shape, F32)], share)
    total = lax.all_to_all(share, "graph", 0, 0).reshape(units, lanes)
    shapes = [(value.shape, F32) for value in (ones[0], w_two, threes[0])]
    found = call(
        moments_kernel,
        shapes * 3 + [((2, 6), F32)],
        total,
        *(group[0] for group in (ones, twos, threes)),
        *(group[1] for group in (ones, twos, threes)),
        *(group[2] for group in (ones, twos, threes)),
    )
    found_norms = lax.psum(found[9], "mp")
    stepped = call(
        steps_kernel,
        [(shape, F32, 0) for shape, kind in shapes]
        + [(shape, BF16, 0) for shape, kind in shapes]
        + [((2, 6), F32, 0)],
        found_norms,
        ones[0],
        w_two,
        threes[0],
        *found[6:9],
    )

    def restored(values):
        return (
            jnp.transpose(values[0], (0, 2, 1)),
            values[1],
            jnp.transpose(values[2], (1, 2, 0)),
        )

    return (
        loss.reshape(()),
        *restored(stepped[0:3]),
        *restored(stepped[3:6]),
        *restored(found[0:3]),
        *restored(found[3:6]),
        stepped[6],
        table_new,
    )


def local_wide(
    features,
    edge_dst,
    degree,
    fresh,
    seed_mask,
    labels,
    table,
    w_one,
    w_two,
    w_three,
    m_one,
    v_one,
    m_two,
    v_two,
    m_three,
    v_three,
):
    devices = lax.axis_size("graph")
    me = lax.axis_index("graph")
    mine = lax.axis_index("mp")
    nodes, in_units = features.shape
    fanout = edge_dst.shape[1]
    units = w_one.shape[2]
    hidden = w_two.shape[2]
    classes = w_three.shape[2]
    degrees = degree.astype(F32)[None, :]
    is_fresh = (fresh > 0)[None, :]
    valid = seed_mask.astype(F32)[None, :]

    def gather(block):
        return lax.all_gather(block, "graph", axis=1, tiled=True)

    dst_rows = edge_dst.T
    feature_rows = features.T
    first_rows = in_units + 2 * fanout + 1
    first_message = pad_rows(
        jnp.concatenate(
            [
                feature_rows,
                (dst_rows // DIGIT).astype(BF16),
                (dst_rows % DIGIT).astype(BF16),
                valid.astype(BF16),
            ],
            axis=0,
        ),
        -(-first_rows // 16) * 16,
    )
    firsts = gather(first_message)
    low_one = jnp.transpose(w_one.astype(BF16), (0, 2, 1))
    low_two = w_two.astype(BF16)
    low_three = w_three.astype(BF16)
    wide_in = -(-in_units // 128) * 128
    wide_class = -(-classes // 64) * 64
    own_message = jnp.concatenate(
        [
            table[0].astype(BF16),
            pad_lanes(low_one[0], wide_in),
            pad_lanes(low_one[1], wide_in),
            low_two[0],
            low_two[1],
            pad_lanes(low_three[0], wide_class),
            pad_lanes(low_three[1], wide_class),
        ],
        axis=1,
    )
    whole = lax.all_gather(own_message, "mp", axis=0, tiled=True)
    cuts = [nodes, wide_in, wide_in, hidden, hidden, wide_class, wide_class]
    pieces = []
    at = 0
    for cut in cuts:
        pieces.append(whole[:, at : at + cut])
        at += cut
    old_one, all_one_self, all_one_near = pieces[0], pieces[1][:, :in_units], pieces[2][:, :in_units]
    all_two_self, all_two_near = pieces[3], pieces[4]
    all_three_self, all_three_near = pieces[5][:, :classes], pieces[6][:, :classes]

    all_features = firsts[:in_units]
    high = firsts[in_units : in_units + fanout].astype(F32)
    low = firsts[in_units + fanout : in_units + 2 * fanout].astype(F32)
    all_dst = (high * DIGIT + low).astype(jnp.int32)
    seed_count = jnp.sum(firsts[in_units + 2 * fanout].astype(F32))

    def spread(all_rows):
        def step(total, block):
            rows = lax.dynamic_slice_in_dim(all_rows, block * nodes, nodes, 1)
            dst = lax.dynamic_slice_in_dim(all_dst, block * nodes, nodes, 1)
            return total + nt(rows, count_block(dst, me * nodes, nodes)), None

        start = jnp.zeros((all_rows.shape[0], nodes), F32)
        return lax.scan(step, start, jnp.arange(devices, dtype=jnp.int32))[0]

    def collect(all_rows):
        def step(total, block):
            rows = lax.dynamic_slice_in_dim(all_rows, block * nodes, nodes, 1)
            return total + nn(rows, count_block(dst_rows, block * nodes, nodes)), None

        start = jnp.zeros((all_rows.shape[0], nodes), F32)
        return lax.scan(step, start, jnp.arange(devices, dtype=jnp.int32))[0]

    def mine_of(rows):
        return lax.dynamic_slice_in_dim(rows, mine * units, units, 0)

    near_one = nn(all_one_near, all_features).astype(BF16)
    in_sums = spread(all_features)
    pre_one = nn(all_one_self, feature_rows) + spread(near_one) / degrees
    input_two = jnp.where(is_fresh, jax.nn.relu(pre_one).astype(BF16), old_one)
    pre_one = mine_of(pre_one)
    hidden_one = jnp.where(is_fresh, jax.nn.relu(pre_one), table[0])
    near_two = nn(low_two[1], input_two).astype(BF16)
    pre_two = nn(low_two[0], input_two) + spread(gather(near_two)) / degrees
    hidden_two = jnp.where(is_fresh, jax.nn.relu(pre_two), table[1])
    low_hidden = hidden_two.astype(BF16)
    input_three = lax.all_gather(low_hidden, "mp", axis=0, tiled=True)
    near_three = tn(all_three_near, input_three).astype(BF16)
    class_rows = -(-(classes + 1) // 16) * 16
    sums = spread(gather(pad_rows(near_three, class_rows)))[:classes]
    logits = tn(all_three_self, input_three) + sums / degrees
    log_probs = jax.nn.log_softmax(logits, axis=0)
    targets = (lax.broadcasted_iota(jnp.int32, logits.shape, 0) == labels[None, :]).astype(F32)
    per_seed = -(
        0.9 * jnp.sum(targets * log_probs, axis=0, keepdims=True)
        + 0.1 * jnp.mean(log_probs, axis=0, keepdims=True)
    )
    loss_part = jnp.sum(per_seed * valid)

    grad_logits = valid * (jnp.exp(log_probs) - 0.9 * targets - 0.1 / classes) / seed_count
    low_grad_three = grad_logits.astype(BF16)
    edge_three = (low_grad_three.astype(F32) / degrees).astype(BF16)
    lanes = lax.broadcasted_iota(jnp.int32, (1, nodes), 1)
    loss_high = kept(loss_part)
    loss_mid = kept(loss_part - loss_high)
    loss_row = jnp.where(
        lanes == 0,
        loss_high,
        jnp.where(
            lanes == 1, loss_mid, jnp.where(lanes == 2, loss_part - loss_high - loss_mid, 0.0)
        ),
    ).astype(BF16)
    thirds = gather(pad_rows(jnp.concatenate([edge_three, loss_row], axis=0), class_rows))
    loss_value = jnp.sum(thirds[classes].astype(F32)) / seed_count
    near_grad_three = collect(thirds)[:classes].astype(BF16)
    grads_three = [nt(low_hidden, low_grad_three), nt(low_hidden, near_grad_three)]
    grad_hidden_two = nn(low_three[0], low_grad_three) + nn(low_three[1], near_grad_three)
    low_grad_two = jnp.where(is_fresh & (pre_two > 0), grad_hidden_two, 0.0).astype(BF16)
    edge_two = (low_grad_two.astype(F32) / degrees).astype(BF16)
    near_grad_two = collect(gather(edge_two)).astype(BF16)
    grads_two = [nt(low_grad_two, input_two), nt(near_grad_two, input_two)]
    both = lax.all_gather(
        jnp.concatenate([low_grad_two, near_grad_two], axis=1), "mp", axis=0, tiled=True
    )
    columns_self = lax.dynamic_slice_in_dim(all_two_self, mine * units, units, 1)
    columns_near = lax.dynamic_slice_in_dim(all_two_near, mine * units, units, 1)
    grad_hidden_one = tn(columns_self, both[:, :nodes]) + tn(columns_near, both[:, nodes:])
    low_grad_one = jnp.where(is_fresh & (pre_one > 0), grad_hidden_one, 0.0).astype(BF16)
    edge_one = (low_grad_one.astype(F32) / degrees).astype(BF16)
    sums_high, sums_low = in_two(in_sums)
    grads_one = [
        nt(low_grad_one, feature_rows),
        nt(edge_one, sums_high) + nt(edge_one, sums_low),
    ]

    partial = jnp.concatenate(
        [pad_lanes(g, wide_in) for g in grads_one]
        + grads_two
        + [pad_lanes(g, wide_class) for g in grads_three],
        axis=1,
    )
    share = partial.reshape(devices, units // devices, partial.shape[1])
    share = jnp.sum(lax.all_to_all(share, "graph", 0, 0), axis=0)
    share = jnp.broadcast_to(share[None], (devices,) + share.shape)
    total = lax.all_to_all(share, "graph", 0, 0).reshape(partial.shape)
    at = 0
    pieces = []
    for cut, use in (
        (wide_in, in_units),
        (wide_in, in_units),
        (hidden, hidden),
        (hidden, hidden),
        (wide_class, classes),
        (wide_class, classes),
    ):
        pieces.append(total[:, at : at + use])
        at += cut
    grad_one = jnp.stack([pieces[0].T, pieces[1].T])
    grad_two = jnp.stack(pieces[2:4])
    grad_three = jnp.stack(pieces[4:6])

    one_parts = lamb_parts(w_one, m_one, v_one, grad_one)
    two_parts = lamb_parts(w_two, m_two, v_two, grad_two)
    three_parts = lamb_parts(w_three, m_three, v_three, grad_three)

    def squares(values):
        return jnp.concatenate([jnp.sum(v * v, axis=(1, 2)) for v in values])

    norms = jnp.sqrt(
        lax.psum(
            jnp.stack(
                [
                    squares([w_one, w_two, w_three]),
                    squares([one_parts[2], two_parts[2], three_parts[2]]),
                ]
            ),
            "mp",
        )
    )
    ratios = (norms[0] / norms[1])[:, None, None]
    one_new = w_one - 0.5 * ratios[0:2] * one_parts[2]
    two_new = w_two - 0.5 * ratios[2:4] * two_parts[2]
    three_new = w_three - 0.5 * ratios[4:6] * three_parts[2]
    table_new = jnp.stack([hidden_one, hidden_two], axis=0)
    return (
        loss_value,
        one_new,
        two_new,
        three_new,
        one_new.astype(BF16),
        two_new.astype(BF16),
        three_new.astype(BF16),
        one_parts[0],
        two_parts[0],
        three_parts[0],
        one_parts[1],
        two_parts[1],
        three_parts[1],
        norms,
        table_new,
    )


def solution(mesh):
    in_specs = (
        P("graph", None),
        P("graph", None),
        P("graph"),
        P("graph"),
        P("graph"),
        P("graph"),
        P(None, "mp", "graph"),
        P(None, None, "mp"),
        P(None, "mp", None),
        P(None, "mp", None),
        P(None, None, "mp"),
        P(None, None, "mp"),
        P(None, "mp", None),
        P(None, "mp", None),
        P(None, "mp", None),
        P(None, "mp", None),
    )
    out_specs = (
        P(),
        P(None, None, "mp"),
        P(None, "mp", None),
        P(None, "mp", None),
        P(None, None, "mp"),
        P(None, "mp", None),
        P(None, "mp", None),
        P(None, None, "mp"),
        P(None, "mp", None),
        P(None, "mp", None),
        P(None, None, "mp"),
        P(None, "mp", None),
        P(None, "mp", None),
        P(),
        P(None, "mp", "graph"),
    )
    axes = mesh.shape["graph"], mesh.shape["mp"]
    few = axes[0] <= DIRECT_MOST and all(size & (size - 1) == 0 for size in axes)
    local = local_direct if few else local_wide
    return jax.shard_map(local, mesh=mesh, in_specs=in_specs, out_specs=out_specs, check_vma=False)
```

```python
import jax
import jax.numpy as jnp
from jax import lax
from jax.experimental import pallas as pl
from jax.experimental.pallas import tpu as pltpu
from jax.sharding import PartitionSpec as P

STEP = 3
F32 = jnp.float32
BF16 = jnp.bfloat16
DIGIT = 256
DIRECT_MOST = 8


def nt(left, right):
    return lax.dot_general(left, right, (((1,), (1,)), ((), ())), preferred_element_type=F32)


def nn(left, right):
    return lax.dot_general(left, right, (((1,), (0,)), ((), ())), preferred_element_type=F32)


def tn(left, right):
    return lax.dot_general(left, right, (((0,), (0,)), ((), ())), preferred_element_type=F32)


def kept(value):
    return lax.reduce_precision(value, 8, 7)


def in_two(value):
    high = kept(value)
    return high.astype(BF16), (value - high).astype(BF16)


def count_block(dst_rows, first, size):
    ids = lax.broadcasted_iota(jnp.int32, (size, dst_rows.shape[1]), 0) + first
    total = (ids == dst_rows[0:1]).astype(F32)
    for slot in range(1, dst_rows.shape[0]):
        total = total + (ids == dst_rows[slot : slot + 1]).astype(F32)
    return total.astype(BF16)


def pad_rows(value, rows):
    return jnp.pad(value, ((0, rows - value.shape[0]), (0, 0)))


def pad_lanes(value, lanes):
    return jnp.pad(value, ((0, 0), (0, lanes - value.shape[1])))


def lamb_parts(weights, first, second, grad):
    correction = 1.0 - 0.5**STEP
    first_new = 0.5 * first + 0.5 * grad
    second_new = 0.5 * second + 0.5 * grad * grad
    update = first_new / correction / (jnp.sqrt(second_new / correction) + 1e-06) + 0.01 * weights
    return (first_new, second_new, update)


VMEM_BYTES = 24 * 2**20


def call(kernel, outs, *operands, scratch=(), held=True):
    if held:
        operands = [pltpu.with_memory_space_constraint(value, pltpu.VMEM) for value in operands]
    space = pl.BlockSpec(memory_space=pltpu.VMEM)
    found = pl.pallas_call(
        kernel,
        out_shape=[
            jax.ShapeDtypeStruct(*out[:2]) if len(out) > 2 else pltpu.VMEM(*out) for out in outs
        ],
        in_specs=[space] * len(operands),
        out_specs=[space] * len(outs),
        scratch_shapes=[pltpu.VMEM(*each) for each in scratch],
        compiler_params=pltpu.CompilerParams(vmem_limit_bytes=VMEM_BYTES),
    )(*operands)
    return found


def over(row, value):
    return jnp.broadcast_to(row, value.shape)


def arrange(blocks, held):
    half = (len(blocks) - 1) // 2
    core = lax.axis_index("mp") & 1
    held[0] = blocks[0][...]
    for step in range(1, half):
        held[step + half * core] = blocks[step][...]
        held[step + half - half * core] = blocks[half + step][...]
    held[half] = blocks[half][...] + blocks[2 * half][...]


def messages_kernel(
    features, edges, degree, fresh, valid, labels, table, one, two, three, *outs
):
    first, own, facts, edges_kept, table_kept = outs
    for place, fact in enumerate((degree, fresh, valid, labels)):
        facts[place : place + 1] = fact[...].astype(F32)
    edges_kept[...] = edges[...]
    table_kept[...] = table[...]
    in_units, nodes = features.shape
    fanout = edges.shape[0]
    units, hidden = two.shape[1:]
    wide_in = -(-in_units // 128) * 128
    classes = three.shape[0]
    rows = first.shape[0]
    dst = edges[...]
    high = dst // DIGIT
    tail = [high, dst - high * DIGIT, valid[...]]
    used = in_units + 2 * fanout + 1
    whole = jnp.concatenate(
        [features[...].astype(F32)]
        + [part.astype(F32) for part in tail]
        + [jnp.zeros((rows - used, nodes), F32)],
        axis=0,
    )
    first[...] = whole.astype(BF16)
    own[:, :nodes] = table[0].astype(BF16)
    at = nodes
    blank = jnp.zeros((units, wide_in - in_units), F32)
    for which in range(2):
        own[:, at : at + wide_in] = jnp.concatenate([one[which], blank], axis=1).astype(BF16)
        at += wide_in
    for which in range(2):
        own[:, at : at + hidden] = two[which].astype(BF16)
        at += hidden
    pair = jnp.concatenate([three[:, 0, :], three[:, 1, :]], axis=1)
    pair = jnp.concatenate([pair, jnp.zeros((units - classes, 2 * units), F32)], axis=0).T
    turned = jnp.concatenate([pair[:units], pair[units:]], axis=1)
    own[:, at : at + 2 * units] = turned.astype(BF16)


def weights_kernel(*refs):
    count = len(refs) - 8
    blocks = refs[:count]
    (edges, old, one, two_turned, three_turned, back, whole_two, whole_three) = refs[count:]
    units = blocks[0].shape[0]
    mine = lax.axis_index("mp")
    nodes = old.shape[1]
    span = one.shape[1]
    hidden = whole_two.shape[1] // 2
    for step, block in enumerate(blocks):
        place = pl.ds(pl.multiple_of((mine ^ step) * units, units), units)
        old[place, :] = block[:, :nodes]
        one[place, :] = block[:, nodes : nodes + span]
        whole_two[place, :] = block[:, nodes + span : nodes + span + 2 * hidden].astype(F32)
        whole_three[place, :] = block[:, nodes + span + 2 * hidden :].astype(F32)
    three_turned[...] = whole_three[...].T.astype(BF16)
    turned = whole_two[...].T
    whole_two_turned = turned.reshape(2, hidden, hidden)
    for which in range(2):
        part = whole_two_turned[which]
        picked = part[:units]
        for step in range(1, hidden // units):
            picked = jnp.where(mine == step, part[step * units : (step + 1) * units], picked)
        two_turned[:, which * hidden : (which + 1) * hidden] = picked.astype(BF16)
    me = lax.axis_index("graph")
    for step in range(back.shape[0] // nodes):
        counts = count_block(edges, (me ^ step) * nodes, nodes)
        back[step * nodes : (step + 1) * nodes, :] = counts


def one_kernel(in_units, fanout, *refs):
    count = len(refs) - 15
    blocks = refs[:count]
    (facts, table, old, one, own) = refs[count : count + 5]
    (ahead, in_sums, gate, hidden_one, input_two, own_two, near_two, seeds) = refs[
        count + 5 : count + 13
    ]
    pre, held = refs[count + 13 :]
    nodes = facts.shape[1]
    rows = blocks[0].shape[0]
    units, hidden = own_two.shape[0], input_two.shape[0]
    me = lax.axis_index("graph")
    mine = lax.axis_index("mp")
    wide = one.shape[1] // 2
    one_self, one_near = one[:, :rows], one[:, wide : wide + rows]
    base = in_units // 16 * 16
    totals = None
    sums = None
    seed_rows = None
    arrange(blocks, held)
    for step in range(held.shape[0]):
        value = held[step]
        tail = held[step, base:, :].astype(F32)
        at = in_units - base
        digits = tail[at : at + fanout] * DIGIT + tail[at + fanout : at + 2 * fanout]
        seed_row = tail[at + 2 * fanout : at + 2 * fanout + 1]
        counts = count_block(digits.astype(jnp.int32), me * nodes, nodes)
        ahead[:, step * nodes : (step + 1) * nodes] = counts
        near = nn(one_near, value).astype(BF16)
        total, part = nt(near, counts), nt(value, counts)
        totals = total if totals is None else totals + total
        sums = part if sums is None else sums + part
        seed_rows = seed_row if seed_rows is None else seed_rows + seed_row
    in_sums[...] = sums
    seeds[...] = jnp.broadcast_to(jnp.sum(seed_rows, axis=1, keepdims=True), seeds.shape)
    value = nn(one_self, blocks[0][...]) + totals / over(facts[0:1], totals)
    pre[...] = value
    keep = over(facts[1:2], value) > 0
    inputs = jnp.where(keep, jnp.maximum(value, 0.0), old[...].astype(F32)).astype(BF16)
    input_two[...] = inputs
    mine_pre = pre[pl.ds(pl.multiple_of(mine * units, units), units), :]
    keep = over(facts[1:2], mine_pre) > 0
    hidden_one[...] = jnp.where(keep, jnp.maximum(mine_pre, 0.0), table[0])
    gate[...] = jnp.where(keep, jnp.where(mine_pre > 0, 1.0, 0.0), 0.0)
    at = nodes + 2 * wide
    own_two[...] = nn(own[:, at : at + hidden], inputs)
    near_two[...] = nn(own[:, at + hidden : at + 2 * hidden], inputs).astype(BF16)


def summed(blocks, counts, product):
    nodes = blocks[0].shape[1]
    total = None
    for step, block in enumerate(blocks):
        part = product(block[...], counts(step, nodes))
        total = part if total is None else total + part
    return total


def two_kernel(*refs):
    count = len(refs) - 8
    blocks = refs[:count]
    (ahead, own_two, facts, table, hidden_one) = refs[count : count + 5]
    (table_new, low_hidden, gate) = refs[count + 5 :]
    sums = summed(blocks, lambda s, n: ahead[:, s * n : (s + 1) * n], nt)
    value = own_two[...] + sums / over(facts[0:1], sums)
    keep = over(facts[1:2], value) > 0
    hidden = jnp.where(keep, jnp.maximum(value, 0.0), table[1])
    table_new[0] = hidden_one[...]
    table_new[1] = hidden
    low_hidden[...] = hidden.astype(BF16)
    gate[...] = jnp.where(keep, jnp.where(value > 0, 1.0, 0.0), 0.0)


def three_kernel(*refs):
    count = len(refs) - 4
    blocks, (turned, own, near, whole) = refs[:count], refs[count:]
    units = blocks[0].shape[0]
    mine = lax.axis_index("mp")
    for step, block in enumerate(blocks):
        whole[pl.ds(pl.multiple_of((mine ^ step) * units, units), units), :] = block[...]
    both = nn(turned[...], whole[...])
    rows = own.shape[0]
    own[...] = both[:rows]
    near[...] = both[turned.shape[0] // 2 : turned.shape[0] // 2 + rows].astype(BF16)


def loss_kernel(classes, *refs):
    count = len(refs) - 7
    (ahead, own, facts, seeds, low_grad, message, held) = refs[count:]
    arrange(refs[:count], held)
    blocks = [held.at[step] for step in range(held.shape[0])]
    sums = summed(blocks, lambda s, n: ahead[:, s * n : (s + 1) * n], nt)
    degrees = over(facts[0:1], sums)
    logits = own[...] + sums / degrees
    row = lax.broadcasted_iota(jnp.int32, logits.shape, 0)
    real = row < classes
    logits = jnp.where(real, logits, -1e30)
    shifted = logits - over(jnp.max(logits, axis=0, keepdims=True), logits)
    scale = jnp.log(jnp.sum(jnp.exp(shifted), axis=0, keepdims=True))
    log_probs = jnp.where(real, shifted - over(scale, logits), 0.0)
    targets = jnp.where(row.astype(F32) == over(facts[3:4], logits), 1.0, 0.0)
    chosen = jnp.sum(targets * log_probs, axis=0, keepdims=True)
    per_seed = -(0.9 * chosen + 0.1 * (jnp.sum(log_probs, axis=0, keepdims=True) / classes))
    weight = facts[2:3]
    loss = jnp.sum(per_seed * weight, axis=1, keepdims=True)
    total = over(seeds[0:1, 0:1], logits)
    grad = over(weight, logits) * (jnp.exp(log_probs) - 0.9 * targets - 0.1 / classes) / total
    low = jnp.where(real, grad, 0.0).astype(BF16)
    low_grad[...] = low
    edge = low.astype(F32) / degrees
    lane = lax.broadcasted_iota(jnp.int32, logits.shape, 1)
    high = loss.astype(BF16).astype(F32)
    middle = (loss - high).astype(BF16).astype(F32)
    rest = loss - high - middle
    digits = jnp.where(
        lane == 0,
        over(high, logits),
        jnp.where(lane == 1, over(middle, logits), jnp.where(lane == 2, over(rest, logits), 0.0)),
    )
    message[...] = jnp.where(real, edge, jnp.where(row == classes, digits, 0.0)).astype(BF16)


def back_three_kernel(classes, *refs):
    count = len(refs) - 12
    (back, low_grad, low_hidden, own_message, gate, facts, seeds) = refs[count : count + 7]
    (loss, grads, low_two, edge_two, held) = refs[count + 7 :]
    arrange(refs[:count], held)
    blocks = [held.at[step] for step in range(held.shape[0])]
    rows = blocks[0].shape[0]
    units = low_hidden.shape[0]
    sums = summed(blocks, lambda s, n: back[s * n : (s + 1) * n, :], nn)
    near = sums.astype(BF16)
    base = classes // 16 * 16
    tail = None
    for block in blocks:
        part = block[base:, :].astype(F32)
        tail = part if tail is None else tail + part
    parts = jnp.sum(tail[classes - base : classes - base + 1, :128], axis=1, keepdims=True)
    loss[...] = parts / seeds[0:1, 0:1]
    low = low_grad[...]
    at = own_message.shape[1] - 2 * units
    value = nn(own_message[:, at : at + rows], low)
    value = value + nn(own_message[:, at + units : at + units + rows], near)
    value = (value * gate[...]).astype(BF16)
    low_two[...] = value
    edge_two[...] = (value.astype(F32) / over(facts[0:1], gate)).astype(BF16)
    grads[...] = jnp.zeros(grads.shape, F32)
    grads[:rows, :units] = nt(low, low_hidden[...])
    grads[:rows, units:] = nt(near, low_hidden[...])


def back_two_kernel(*refs):
    count = len(refs) - 2
    blocks, (back, near) = refs[:count], refs[count:]
    near[...] = summed(blocks, lambda s, n: back[s * n : (s + 1) * n, :], nn).astype(BF16)


def back_one_kernel(peers, *refs):
    lows, nears = refs[:peers], refs[peers : 2 * peers]
    (two_turned, gate, facts, first, in_sums, input_two, grads_three) = refs[
        2 * peers : 2 * peers + 7
    ]
    (partial, whole_low, whole_near) = refs[2 * peers + 7 :]
    units = lows[0].shape[0]
    hidden = units * peers
    rows = first.shape[0]
    wide = -(-rows // 128) * 128
    mine = lax.axis_index("mp")
    for step in range(peers):
        place = pl.ds(pl.multiple_of((mine ^ step) * units, units), units)
        whole_low[place, :] = lows[step][...]
        whole_near[place, :] = nears[step][...]
    value = nn(two_turned[:, :hidden], whole_low[...])
    value = value + nn(two_turned[:, hidden:], whole_near[...])
    low = (value * gate[...]).astype(BF16)
    edge = (low.astype(F32) / over(facts[0:1], gate)).astype(BF16)
    sums = in_sums[...]
    high = sums.astype(BF16)
    rest = (sums - high.astype(F32)).astype(BF16)
    blank = jnp.zeros((units, wide - rows), F32)
    partial[:, :wide] = jnp.concatenate([nt(low, first[...]), blank], axis=1)
    partial[:, wide : 2 * wide] = jnp.concatenate([nt(edge, high) + nt(edge, rest), blank], axis=1)
    at = 2 * wide
    partial[:, at : at + hidden] = nt(lows[0][...], input_two[...])
    at += hidden
    partial[:, at : at + hidden] = nt(nears[0][...], input_two[...])
    at += hidden
    partial[:, at:] = grads_three[...]


def add_kernel(shares, out):
    total = shares[0]
    for step in range(1, shares.shape[0]):
        total = total + shares[step]
    for step in range(out.shape[0]):
        out[step] = total


def pieces_of(total, one, two, three):
    in_units, hidden = one.shape[2], two.shape[2]
    classes, units = three.shape[0], three.shape[2]
    wide = -(-in_units // 128) * 128
    at = 2 * wide + 2 * hidden
    return [
        (0, lambda ref: (ref, 0), total[:, :in_units]),
        (0, lambda ref: (ref, 1), total[:, wide : wide + in_units]),
        (1, lambda ref: (ref, 0), total[:, 2 * wide : 2 * wide + hidden]),
        (1, lambda ref: (ref, 1), total[:, 2 * wide + hidden : at]),
        (2, lambda ref: (ref, (slice(None), 0, slice(None))), total[:classes, at : at + units]),
        (2, lambda ref: (ref, (slice(None), 1, slice(None))), total[:classes, at + units :]),
    ]


def moments_kernel(total, *refs):
    weights, firsts, seconds = refs[0:3], refs[3:6], refs[6:9]
    firsts_new, seconds_new, updates = refs[9:12], refs[12:15], refs[15:18]
    squares = refs[18]
    row = lax.broadcasted_iota(jnp.int32, squares.shape, 0)
    lane = lax.broadcasted_iota(jnp.int32, squares.shape, 1)
    found = jnp.zeros(squares.shape, F32)
    for place, (which, at, grad) in enumerate(pieces_of(total[...], *weights)):
        index = at(None)[1]
        weight = weights[which][index]
        parts = lamb_parts(weight, firsts[which][index], seconds[which][index], grad)
        firsts_new[which][index] = parts[0]
        seconds_new[which][index] = parts[1]
        updates[which][index] = parts[2]
        for line, value in ((0, weight), (1, parts[2])):
            square = jnp.sum(value * value, axis=0, keepdims=True)
            square = jnp.sum(square, axis=1, keepdims=True)
            here = jnp.where(row == line, jnp.where(lane == place, 1.0, 0.0), 0.0)
            found = found + here * over(square, found)
    squares[...] = found


def steps_kernel(squares, *refs):
    weights, updates = refs[0:3], refs[3:6]
    news, copies, norms = refs[6:9], refs[9:12], refs[12]
    roots = jnp.sqrt(squares[...])
    norms[...] = roots
    for place in range(6):
        which = place // 2
        index = (slice(None), place % 2, slice(None)) if which == 2 else place % 2
        ratio = roots[0:1, place : place + 1] / roots[1:2, place : place + 1]
        weight = weights[which][index]
        new = weight - 0.5 * over(ratio, weight) * updates[which][index]
        news[which][index] = new
        copies[which][index] = new.astype(BF16)


def local_direct(
    features,
    edge_dst,
    degree,
    fresh,
    seed_mask,
    labels,
    table,
    w_one,
    w_two,
    w_three,
    m_one,
    v_one,
    m_two,
    v_two,
    m_three,
    v_three,
):
    devices = lax.axis_size("graph")
    peers = lax.axis_size("mp")
    nodes, in_units = features.shape
    fanout = edge_dst.shape[1]
    units = w_one.shape[2]
    hidden = w_two.shape[2]
    classes = w_three.shape[2]
    wide_in = -(-in_units // 128) * 128
    first_rows = -(-(in_units + 2 * fanout + 1) // 16) * 16
    class_rows = -(-(classes + 1) // 16) * 16
    line = (1, nodes)
    degree, fresh, valid, labels = [
        value.reshape(line) for value in (degree, fresh, seed_mask, labels)
    ]
    edges = edge_dst.T
    ones = [jnp.transpose(value, (0, 2, 1)) for value in (w_one, m_one, v_one)]
    twos = [w_two, m_two, v_two]
    threes = [jnp.transpose(value, (2, 0, 1)) for value in (w_three, m_three, v_three)]

    def exchange(block, axis, size):
        return [block] + [
            lax.ppermute(block, axis, [(i, i ^ step) for i in range(size)])
            for step in range(1, size)
        ]

    def gather(block):
        return exchange(block, "graph", devices)

    def gather_shared(block):
        half = devices // 2
        got = []
        for step in range(1, half + 1):
            pairs = [
                (i * peers + j, (i ^ (step + half * (j & 1))) * peers + j)
                for i in range(devices)
                for j in range(peers)
                if step + half * (j & 1) < devices
            ]
            got.append(lax.ppermute(block, ("graph", "mp"), pairs))
        swaps = [(j, j ^ 1) for j in range(peers)]
        return [block] + got + [lax.ppermute(part, "mp", swaps) for part in got]

    own_lanes = nodes + 2 * wide_in + 2 * hidden + 2 * units
    first, own, facts, edges, table = call(
        messages_kernel,
        [
            ((first_rows, nodes), BF16),
            ((units, own_lanes), BF16),
            ((4, nodes), F32),
            (edges.shape, jnp.int32),
            (table.shape, F32),
        ],
        features.T,
        edges,
        degree,
        fresh,
        valid,
        labels,
        table,
        ones[0],
        w_two,
        threes[0],
        held=False,
    )
    firsts = gather_shared(first)
    owns = exchange(own, "mp", peers)
    old, one, two_turned, three_turned, back = call(
        weights_kernel,
        [
            ((hidden, nodes), BF16),
            ((hidden, 2 * wide_in), BF16),
            ((units, 2 * hidden), BF16),
            ((2 * units, hidden), BF16),
            ((devices * nodes, nodes), BF16),
        ],
        *owns,
        edges,
        scratch=[((hidden, 2 * hidden), F32), ((hidden, 2 * units), F32)],
    )
    ahead, in_sums, gate_one, hidden_one, input_two, own_two, near_two, seeds = call(
        lambda *refs: one_kernel(in_units, fanout, *refs),
        [
            ((nodes, devices * nodes), BF16),
            ((first_rows, nodes), F32),
            ((units, nodes), F32),
            ((units, nodes), F32),
            ((hidden, nodes), BF16),
            ((units, nodes), F32),
            ((units, nodes), BF16),
            ((8, 128), F32),
        ],
        *firsts,
        facts,
        table,
        old,
        one,
        own,
        scratch=[((hidden, nodes), F32), ((devices, first_rows, nodes), BF16)],
    )
    table_new, low_hidden, gate_two = call(
        two_kernel,
        [((2, units, nodes), F32), ((units, nodes), BF16), ((units, nodes), F32)],
        *gather(near_two),
        ahead,
        own_two,
        facts,
        table,
        hidden_one,
    )
    own_three, near_three = call(
        three_kernel,
        [((class_rows, nodes), F32), ((class_rows, nodes), BF16)],
        *exchange(low_hidden, "mp", peers),
        three_turned,
        scratch=[((hidden, nodes), BF16)],
    )
    low_three, message = call(
        lambda *refs: loss_kernel(classes, *refs),
        [((class_rows, nodes), BF16), ((class_rows, nodes), BF16)],
        *gather_shared(near_three),
        ahead,
        own_three,
        facts,
        seeds,
        scratch=[((devices, class_rows, nodes), BF16)],
    )
    loss, grads_three, low_two, edge_two = call(
        lambda *refs: back_three_kernel(classes, *refs),
        [
            ((1, 1), F32, 0),
            ((units, 2 * units), F32),
            ((units, nodes), BF16),
            ((units, nodes), BF16),
        ],
        *gather_shared(message),
        back,
        low_three,
        low_hidden,
        own,
        gate_two,
        facts,
        seeds,
        scratch=[((devices, class_rows, nodes), BF16)],
    )
    edges_two = gather(edge_two)
    lows = exchange(low_two, "mp", peers)
    (near_grad,) = call(back_two_kernel, [((units, nodes), BF16)], *edges_two, back)
    nears = exchange(near_grad, "mp", peers)
    lanes = 2 * wide_in + 2 * hidden + 2 * units
    (partial,) = call(
        lambda *refs: back_one_kernel(peers, *refs),
        [((units, lanes), F32)],
        *lows,
        *nears,
        two_turned,
        gate_one,
        facts,
        first,
        in_sums,
        input_two,
        grads_three,
        scratch=[((hidden, nodes), BF16)] * 2,
    )

    share = partial.reshape(devices, units // devices, lanes)
    share = lax.all_to_all(share, "graph", 0, 0)
    (share,) = call(add_kernel, [(share.shape, F32)], share)
    total = lax.all_to_all(share, "graph", 0, 0).reshape(units, lanes)
    shapes = [(value.shape, F32) for value in (ones[0], w_two, threes[0])]
    found = call(
        moments_kernel,
        [shape + (0,) for shape in shapes * 2] + shapes + [((2, 6), F32)],
        total,
        *(group[0] for group in (ones, twos, threes)),
        *(group[1] for group in (ones, twos, threes)),
        *(group[2] for group in (ones, twos, threes)),
    )
    found_norms = lax.psum(found[9], "mp")
    stepped = call(
        steps_kernel,
        [(shape, F32, 0) for shape, kind in shapes]
        + [(shape, BF16, 0) for shape, kind in shapes]
        + [((2, 6), F32, 0)],
        found_norms,
        ones[0],
        w_two,
        threes[0],
        *found[6:9],
    )

    def restored(values):
        return (
            jnp.transpose(values[0], (0, 2, 1)),
            values[1],
            jnp.transpose(values[2], (1, 2, 0)),
        )

    return (
        loss.reshape(()),
        *restored(stepped[0:3]),
        *restored(stepped[3:6]),
        *restored(found[0:3]),
        *restored(found[3:6]),
        stepped[6],
        table_new,
    )


def local_wide(
    features,
    edge_dst,
    degree,
    fresh,
    seed_mask,
    labels,
    table,
    w_one,
    w_two,
    w_three,
    m_one,
    v_one,
    m_two,
    v_two,
    m_three,
    v_three,
):
    devices = lax.axis_size("graph")
    me = lax.axis_index("graph")
    mine = lax.axis_index("mp")
    nodes, in_units = features.shape
    fanout = edge_dst.shape[1]
    units = w_one.shape[2]
    hidden = w_two.shape[2]
    classes = w_three.shape[2]
    degrees = degree.astype(F32)[None, :]
    is_fresh = (fresh > 0)[None, :]
    valid = seed_mask.astype(F32)[None, :]

    def gather(block):
        return lax.all_gather(block, "graph", axis=1, tiled=True)

    dst_rows = edge_dst.T
    feature_rows = features.T
    first_rows = in_units + 2 * fanout + 1
    first_message = pad_rows(
        jnp.concatenate(
            [
                feature_rows,
                (dst_rows // DIGIT).astype(BF16),
                (dst_rows % DIGIT).astype(BF16),
                valid.astype(BF16),
            ],
            axis=0,
        ),
        -(-first_rows // 16) * 16,
    )
    firsts = gather(first_message)
    low_one = jnp.transpose(w_one.astype(BF16), (0, 2, 1))
    low_two = w_two.astype(BF16)
    low_three = w_three.astype(BF16)
    wide_in = -(-in_units // 128) * 128
    wide_class = -(-classes // 64) * 64
    own_message = jnp.concatenate(
        [
            table[0].astype(BF16),
            pad_lanes(low_one[0], wide_in),
            pad_lanes(low_one[1], wide_in),
            low_two[0],
            low_two[1],
            pad_lanes(low_three[0], wide_class),
            pad_lanes(low_three[1], wide_class),
        ],
        axis=1,
    )
    whole = lax.all_gather(own_message, "mp", axis=0, tiled=True)
    cuts = [nodes, wide_in, wide_in, hidden, hidden, wide_class, wide_class]
    pieces = []
    at = 0
    for cut in cuts:
        pieces.append(whole[:, at : at + cut])
        at += cut
    old_one, all_one_self, all_one_near = pieces[0], pieces[1][:, :in_units], pieces[2][:, :in_units]
    all_two_self, all_two_near = pieces[3], pieces[4]
    all_three_self, all_three_near = pieces[5][:, :classes], pieces[6][:, :classes]

    all_features = firsts[:in_units]
    high = firsts[in_units : in_units + fanout].astype(F32)
    low = firsts[in_units + fanout : in_units + 2 * fanout].astype(F32)
    all_dst = (high * DIGIT + low).astype(jnp.int32)
    seed_count = jnp.sum(firsts[in_units + 2 * fanout].astype(F32))

    def spread(all_rows):
        def step(total, block):
            rows = lax.dynamic_slice_in_dim(all_rows, block * nodes, nodes, 1)
            dst = lax.dynamic_slice_in_dim(all_dst, block * nodes, nodes, 1)
            return total + nt(rows, count_block(dst, me * nodes, nodes)), None

        start = jnp.zeros((all_rows.shape[0], nodes), F32)
        return lax.scan(step, start, jnp.arange(devices, dtype=jnp.int32))[0]

    def collect(all_rows):
        def step(total, block):
            rows = lax.dynamic_slice_in_dim(all_rows, block * nodes, nodes, 1)
            return total + nn(rows, count_block(dst_rows, block * nodes, nodes)), None

        start = jnp.zeros((all_rows.shape[0], nodes), F32)
        return lax.scan(step, start, jnp.arange(devices, dtype=jnp.int32))[0]

    def mine_of(rows):
        return lax.dynamic_slice_in_dim(rows, mine * units, units, 0)

    near_one = nn(all_one_near, all_features).astype(BF16)
    in_sums = spread(all_features)
    pre_one = nn(all_one_self, feature_rows) + spread(near_one) / degrees
    input_two = jnp.where(is_fresh, jax.nn.relu(pre_one).astype(BF16), old_one)
    pre_one = mine_of(pre_one)
    hidden_one = jnp.where(is_fresh, jax.nn.relu(pre_one), table[0])
    near_two = nn(low_two[1], input_two).astype(BF16)
    pre_two = nn(low_two[0], input_two) + spread(gather(near_two)) / degrees
    hidden_two = jnp.where(is_fresh, jax.nn.relu(pre_two), table[1])
    low_hidden = hidden_two.astype(BF16)
    input_three = lax.all_gather(low_hidden, "mp", axis=0, tiled=True)
    near_three = tn(all_three_near, input_three).astype(BF16)
    class_rows = -(-(classes + 1) // 16) * 16
    sums = spread(gather(pad_rows(near_three, class_rows)))[:classes]
    logits = tn(all_three_self, input_three) + sums / degrees
    log_probs = jax.nn.log_softmax(logits, axis=0)
    targets = (lax.broadcasted_iota(jnp.int32, logits.shape, 0) == labels[None, :]).astype(F32)
    per_seed = -(
        0.9 * jnp.sum(targets * log_probs, axis=0, keepdims=True)
        + 0.1 * jnp.mean(log_probs, axis=0, keepdims=True)
    )
    loss_part = jnp.sum(per_seed * valid)

    grad_logits = valid * (jnp.exp(log_probs) - 0.9 * targets - 0.1 / classes) / seed_count
    low_grad_three = grad_logits.astype(BF16)
    edge_three = (low_grad_three.astype(F32) / degrees).astype(BF16)
    lanes = lax.broadcasted_iota(jnp.int32, (1, nodes), 1)
    loss_high = kept(loss_part)
    loss_mid = kept(loss_part - loss_high)
    loss_row = jnp.where(
        lanes == 0,
        loss_high,
        jnp.where(
            lanes == 1, loss_mid, jnp.where(lanes == 2, loss_part - loss_high - loss_mid, 0.0)
        ),
    ).astype(BF16)
    thirds = gather(pad_rows(jnp.concatenate([edge_three, loss_row], axis=0), class_rows))
    loss_value = jnp.sum(thirds[classes].astype(F32)) / seed_count
    near_grad_three = collect(thirds)[:classes].astype(BF16)
    grads_three = [nt(low_hidden, low_grad_three), nt(low_hidden, near_grad_three)]
    grad_hidden_two = nn(low_three[0], low_grad_three) + nn(low_three[1], near_grad_three)
    low_grad_two = jnp.where(is_fresh & (pre_two > 0), grad_hidden_two, 0.0).astype(BF16)
    edge_two = (low_grad_two.astype(F32) / degrees).astype(BF16)
    near_grad_two = collect(gather(edge_two)).astype(BF16)
    grads_two = [nt(low_grad_two, input_two), nt(near_grad_two, input_two)]
    both = lax.all_gather(
        jnp.concatenate([low_grad_two, near_grad_two], axis=1), "mp", axis=0, tiled=True
    )
    columns_self = lax.dynamic_slice_in_dim(all_two_self, mine * units, units, 1)
    columns_near = lax.dynamic_slice_in_dim(all_two_near, mine * units, units, 1)
    grad_hidden_one = tn(columns_self, both[:, :nodes]) + tn(columns_near, both[:, nodes:])
    low_grad_one = jnp.where(is_fresh & (pre_one > 0), grad_hidden_one, 0.0).astype(BF16)
    edge_one = (low_grad_one.astype(F32) / degrees).astype(BF16)
    sums_high, sums_low = in_two(in_sums)
    grads_one = [
        nt(low_grad_one, feature_rows),
        nt(edge_one, sums_high) + nt(edge_one, sums_low),
    ]

    partial = jnp.concatenate(
        [pad_lanes(g, wide_in) for g in grads_one]
        + grads_two
        + [pad_lanes(g, wide_class) for g in grads_three],
        axis=1,
    )
    share = partial.reshape(devices, units // devices, partial.shape[1])
    share = jnp.sum(lax.all_to_all(share, "graph", 0, 0), axis=0)
    share = jnp.broadcast_to(share[None], (devices,) + share.shape)
    total = lax.all_to_all(share, "graph", 0, 0).reshape(partial.shape)
    at = 0
    pieces = []
    for cut, use in (
        (wide_in, in_units),
        (wide_in, in_units),
        (hidden, hidden),
        (hidden, hidden),
        (wide_class, classes),
        (wide_class, classes),
    ):
        pieces.append(total[:, at : at + use])
        at += cut
    grad_one = jnp.stack([pieces[0].T, pieces[1].T])
    grad_two = jnp.stack(pieces[2:4])
    grad_three = jnp.stack(pieces[4:6])

    one_parts = lamb_parts(w_one, m_one, v_one, grad_one)
    two_parts = lamb_parts(w_two, m_two, v_two, grad_two)
    three_parts = lamb_parts(w_three, m_three, v_three, grad_three)

    def squares(values):
        return jnp.concatenate([jnp.sum(v * v, axis=(1, 2)) for v in values])

    norms = jnp.sqrt(
        lax.psum(
            jnp.stack(
                [
                    squares([w_one, w_two, w_three]),
                    squares([one_parts[2], two_parts[2], three_parts[2]]),
                ]
            ),
            "mp",
        )
    )
    ratios = (norms[0] / norms[1])[:, None, None]
    one_new = w_one - 0.5 * ratios[0:2] * one_parts[2]
    two_new = w_two - 0.5 * ratios[2:4] * two_parts[2]
    three_new = w_three - 0.5 * ratios[4:6] * three_parts[2]
    table_new = jnp.stack([hidden_one, hidden_two], axis=0)
    return (
        loss_value,
        one_new,
        two_new,
        three_new,
        one_new.astype(BF16),
        two_new.astype(BF16),
        three_new.astype(BF16),
        one_parts[0],
        two_parts[0],
        three_parts[0],
        one_parts[1],
        two_parts[1],
        three_parts[1],
        norms,
        table_new,
    )


def solution(mesh):
    in_specs = (
        P("graph", None),
        P("graph", None),
        P("graph"),
        P("graph"),
        P("graph"),
        P("graph"),
        P(None, "mp", "graph"),
        P(None, None, "mp"),
        P(None, "mp", None),
        P(None, "mp", None),
        P(None, None, "mp"),
        P(None, None, "mp"),
        P(None, "mp", None),
        P(None, "mp", None),
        P(None, "mp", None),
        P(None, "mp", None),
    )
    out_specs = (
        P(),
        P(None, None, "mp"),
        P(None, "mp", None),
        P(None, "mp", None),
        P(None, None, "mp"),
        P(None, "mp", None),
        P(None, "mp", None),
        P(None, None, "mp"),
        P(None, "mp", None),
        P(None, "mp", None),
        P(None, None, "mp"),
        P(None, "mp", None),
        P(None, "mp", None),
        P(),
        P(None, "mp", "graph"),
    )
    axes = mesh.shape["graph"], mesh.shape["mp"]
    few = axes[0] <= DIRECT_MOST and all(size > 1 and size & (size - 1) == 0 for size in axes)
    local = local_direct if few else local_wide
    return jax.shard_map(local, mesh=mesh, in_specs=in_specs, out_specs=out_specs, check_vma=False)
```

```python
import jax
import jax.numpy as jnp
from jax import lax
from jax.experimental import pallas as pl
from jax.experimental.pallas import tpu as pltpu
from jax.sharding import PartitionSpec as P

STEP = 3
F32 = jnp.float32
BF16 = jnp.bfloat16
DIGIT = 256
DIRECT_MOST = 8


def nt(left, right):
    return lax.dot_general(left, right, (((1,), (1,)), ((), ())), preferred_element_type=F32)


def nn(left, right):
    return lax.dot_general(left, right, (((1,), (0,)), ((), ())), preferred_element_type=F32)


def tn(left, right):
    return lax.dot_general(left, right, (((0,), (0,)), ((), ())), preferred_element_type=F32)


def kept(value):
    return lax.reduce_precision(value, 8, 7)


def in_two(value):
    high = kept(value)
    return high.astype(BF16), (value - high).astype(BF16)


def count_block(dst_rows, first, size):
    ids = lax.broadcasted_iota(jnp.int32, (size, dst_rows.shape[1]), 0) + first
    total = (ids == dst_rows[0:1]).astype(F32)
    for slot in range(1, dst_rows.shape[0]):
        total = total + (ids == dst_rows[slot : slot + 1]).astype(F32)
    return total.astype(BF16)


def pad_rows(value, rows):
    return jnp.pad(value, ((0, rows - value.shape[0]), (0, 0)))


def pad_lanes(value, lanes):
    return jnp.pad(value, ((0, 0), (0, lanes - value.shape[1])))


def lamb_parts(weights, first, second, grad):
    correction = 1.0 - 0.5**STEP
    first_new = 0.5 * first + 0.5 * grad
    second_new = 0.5 * second + 0.5 * grad * grad
    update = first_new / correction / (jnp.sqrt(second_new / correction) + 1e-06) + 0.01 * weights
    return (first_new, second_new, update)


VMEM_BYTES = 24 * 2**20


def call(kernel, outs, *operands, scratch=(), held=True):
    place = pltpu.VMEM if held else pltpu.HBM
    operands = [pltpu.with_memory_space_constraint(value, place) for value in operands]
    space = pl.BlockSpec(memory_space=pltpu.VMEM)
    found = pl.pallas_call(
        kernel,
        out_shape=[
            jax.ShapeDtypeStruct(*out[:2]) if len(out) > 2 else pltpu.VMEM(*out) for out in outs
        ],
        in_specs=[space] * len(operands),
        out_specs=[space] * len(outs),
        scratch_shapes=[pltpu.VMEM(*each) for each in scratch],
        compiler_params=pltpu.CompilerParams(vmem_limit_bytes=VMEM_BYTES),
    )(*operands)
    return found


def over(row, value):
    return jnp.broadcast_to(row, value.shape)


def arrange(blocks, held):
    half = (len(blocks) - 1) // 2
    core = lax.axis_index("mp") & 1
    held[0] = blocks[0][...]
    for step in range(1, half):
        held[step + half * core] = blocks[step][...]
        held[step + half - half * core] = blocks[half + step][...]
    held[half] = blocks[half][...] + blocks[2 * half][...]


def messages_kernel(
    features, edges, degree, fresh, valid, labels, table, one, two, three, *outs
):
    first, own, facts, edges_kept, table_kept = outs
    for place, fact in enumerate((degree, fresh, valid, labels)):
        facts[place : place + 1] = fact[...].astype(F32)
    edges_kept[...] = edges[...]
    table_kept[...] = table[...]
    in_units, nodes = features.shape
    fanout = edges.shape[0]
    units, hidden = two.shape[1:]
    wide_in = -(-in_units // 128) * 128
    classes = three.shape[0]
    rows = first.shape[0]
    dst = edges[...]
    high = dst // DIGIT
    tail = [high, dst - high * DIGIT, valid[...]]
    used = in_units + 2 * fanout + 1
    whole = jnp.concatenate(
        [features[...].astype(F32)]
        + [part.astype(F32) for part in tail]
        + [jnp.zeros((rows - used, nodes), F32)],
        axis=0,
    )
    first[...] = whole.astype(BF16)
    own[:, :nodes] = table[0].astype(BF16)
    at = nodes
    blank = jnp.zeros((units, wide_in - in_units), F32)
    for which in range(2):
        own[:, at : at + wide_in] = jnp.concatenate([one[which], blank], axis=1).astype(BF16)
        at += wide_in
    for which in range(2):
        own[:, at : at + hidden] = two[which].astype(BF16)
        at += hidden
    pair = jnp.concatenate([three[:, 0, :], three[:, 1, :]], axis=1)
    pair = jnp.concatenate([pair, jnp.zeros((units - classes, 2 * units), F32)], axis=0).T
    turned = jnp.concatenate([pair[:units], pair[units:]], axis=1)
    own[:, at : at + 2 * units] = turned.astype(BF16)


def back_kernel(edges, back):
    nodes = edges.shape[1]
    me = lax.axis_index("graph")
    for step in range(back.shape[0] // nodes):
        counts = count_block(edges, (me ^ step) * nodes, nodes)
        back[step * nodes : (step + 1) * nodes, :] = counts


def weights_kernel(*refs):
    count = len(refs) - 6
    blocks = refs[:count]
    (old, one, two_turned, three_turned, whole_two, whole_three) = refs[count:]
    units = blocks[0].shape[0]
    mine = lax.axis_index("mp")
    nodes = old.shape[1]
    span = one.shape[1]
    hidden = whole_two.shape[1] // 2
    for step, block in enumerate(blocks):
        place = pl.ds(pl.multiple_of((mine ^ step) * units, units), units)
        old[place, :] = block[:, :nodes]
        one[place, :] = block[:, nodes : nodes + span]
        whole_two[place, :] = block[:, nodes + span : nodes + span + 2 * hidden].astype(F32)
        whole_three[place, :] = block[:, nodes + span + 2 * hidden :].astype(F32)
    three_turned[...] = whole_three[...].T.astype(BF16)
    turned = whole_two[...].T
    whole_two_turned = turned.reshape(2, hidden, hidden)
    for which in range(2):
        part = whole_two_turned[which]
        picked = part[:units]
        for step in range(1, hidden // units):
            picked = jnp.where(mine == step, part[step * units : (step + 1) * units], picked)
        two_turned[:, which * hidden : (which + 1) * hidden] = picked.astype(BF16)


def one_kernel(in_units, fanout, *refs):
    count = len(refs) - 15
    blocks = refs[:count]
    (facts, table, old, one, own) = refs[count : count + 5]
    (ahead, in_sums, gate, hidden_one, input_two, own_two, near_two, seeds) = refs[
        count + 5 : count + 13
    ]
    pre, held = refs[count + 13 :]
    nodes = facts.shape[1]
    rows = blocks[0].shape[0]
    units, hidden = own_two.shape[0], input_two.shape[0]
    me = lax.axis_index("graph")
    mine = lax.axis_index("mp")
    wide = one.shape[1] // 2
    one_self, one_near = one[:, :rows], one[:, wide : wide + rows]
    base = in_units // 16 * 16
    totals = None
    sums = None
    seed_rows = None
    arrange(blocks, held)
    for step in range(held.shape[0]):
        value = held[step]
        tail = held[step, base:, :].astype(F32)
        at = in_units - base
        digits = tail[at : at + fanout] * DIGIT + tail[at + fanout : at + 2 * fanout]
        seed_row = tail[at + 2 * fanout : at + 2 * fanout + 1]
        counts = count_block(digits.astype(jnp.int32), me * nodes, nodes)
        ahead[:, step * nodes : (step + 1) * nodes] = counts
        near = nn(one_near, value).astype(BF16)
        total, part = nt(near, counts), nt(value, counts)
        totals = total if totals is None else totals + total
        sums = part if sums is None else sums + part
        seed_rows = seed_row if seed_rows is None else seed_rows + seed_row
    in_sums[...] = sums
    seeds[...] = jnp.broadcast_to(jnp.sum(seed_rows, axis=1, keepdims=True), seeds.shape)
    value = nn(one_self, blocks[0][...]) + totals / over(facts[0:1], totals)
    pre[...] = value
    keep = over(facts[1:2], value) > 0
    inputs = jnp.where(keep, jnp.maximum(value, 0.0), old[...].astype(F32)).astype(BF16)
    input_two[...] = inputs
    mine_pre = pre[pl.ds(pl.multiple_of(mine * units, units), units), :]
    keep = over(facts[1:2], mine_pre) > 0
    hidden_one[...] = jnp.where(keep, jnp.maximum(mine_pre, 0.0), table[0])
    gate[...] = jnp.where(keep, jnp.where(mine_pre > 0, 1.0, 0.0), 0.0)
    at = nodes + 2 * wide
    own_two[...] = nn(own[:, at : at + hidden], inputs)
    near_two[...] = nn(own[:, at + hidden : at + 2 * hidden], inputs).astype(BF16)


def summed(blocks, counts, product):
    nodes = blocks[0].shape[1]
    total = None
    for step, block in enumerate(blocks):
        part = product(block[...], counts(step, nodes))
        total = part if total is None else total + part
    return total


def two_kernel(*refs):
    count = len(refs) - 8
    blocks = refs[:count]
    (ahead, own_two, facts, table, hidden_one) = refs[count : count + 5]
    (table_new, low_hidden, gate) = refs[count + 5 :]
    sums = summed(blocks, lambda s, n: ahead[:, s * n : (s + 1) * n], nt)
    value = own_two[...] + sums / over(facts[0:1], sums)
    keep = over(facts[1:2], value) > 0
    hidden = jnp.where(keep, jnp.maximum(value, 0.0), table[1])
    table_new[0] = hidden_one[...]
    table_new[1] = hidden
    low_hidden[...] = hidden.astype(BF16)
    gate[...] = jnp.where(keep, jnp.where(value > 0, 1.0, 0.0), 0.0)


def three_kernel(*refs):
    count = len(refs) - 4
    blocks, (turned, own, near, whole) = refs[:count], refs[count:]
    units = blocks[0].shape[0]
    mine = lax.axis_index("mp")
    for step, block in enumerate(blocks):
        whole[pl.ds(pl.multiple_of((mine ^ step) * units, units), units), :] = block[...]
    both = nn(turned[...], whole[...])
    rows = own.shape[0]
    own[...] = both[:rows]
    near[...] = both[turned.shape[0] // 2 : turned.shape[0] // 2 + rows].astype(BF16)


def loss_kernel(classes, *refs):
    count = len(refs) - 7
    (ahead, own, facts, seeds, low_grad, message, held) = refs[count:]
    arrange(refs[:count], held)
    blocks = [held.at[step] for step in range(held.shape[0])]
    sums = summed(blocks, lambda s, n: ahead[:, s * n : (s + 1) * n], nt)
    degrees = over(facts[0:1], sums)
    logits = own[...] + sums / degrees
    row = lax.broadcasted_iota(jnp.int32, logits.shape, 0)
    real = row < classes
    logits = jnp.where(real, logits, -1e30)
    shifted = logits - over(jnp.max(logits, axis=0, keepdims=True), logits)
    scale = jnp.log(jnp.sum(jnp.exp(shifted), axis=0, keepdims=True))
    log_probs = jnp.where(real, shifted - over(scale, logits), 0.0)
    targets = jnp.where(row.astype(F32) == over(facts[3:4], logits), 1.0, 0.0)
    chosen = jnp.sum(targets * log_probs, axis=0, keepdims=True)
    per_seed = -(0.9 * chosen + 0.1 * (jnp.sum(log_probs, axis=0, keepdims=True) / classes))
    weight = facts[2:3]
    loss = jnp.sum(per_seed * weight, axis=1, keepdims=True)
    total = over(seeds[0:1, 0:1], logits)
    grad = over(weight, logits) * (jnp.exp(log_probs) - 0.9 * targets - 0.1 / classes) / total
    low = jnp.where(real, grad, 0.0).astype(BF16)
    low_grad[...] = low
    edge = low.astype(F32) / degrees
    lane = lax.broadcasted_iota(jnp.int32, logits.shape, 1)
    high = loss.astype(BF16).astype(F32)
    middle = (loss - high).astype(BF16).astype(F32)
    rest = loss - high - middle
    digits = jnp.where(
        lane == 0,
        over(high, logits),
        jnp.where(lane == 1, over(middle, logits), jnp.where(lane == 2, over(rest, logits), 0.0)),
    )
    message[...] = jnp.where(real, edge, jnp.where(row == classes, digits, 0.0)).astype(BF16)


def back_three_kernel(classes, *refs):
    count = len(refs) - 12
    (back, low_grad, low_hidden, own_message, gate, facts, seeds) = refs[count : count + 7]
    (loss, grads, low_two, edge_two, held) = refs[count + 7 :]
    arrange(refs[:count], held)
    blocks = [held.at[step] for step in range(held.shape[0])]
    rows = blocks[0].shape[0]
    units = low_hidden.shape[0]
    sums = summed(blocks, lambda s, n: back[s * n : (s + 1) * n, :], nn)
    near = sums.astype(BF16)
    base = classes // 16 * 16
    tail = None
    for block in blocks:
        part = block[base:, :].astype(F32)
        tail = part if tail is None else tail + part
    parts = jnp.sum(tail[classes - base : classes - base + 1, :128], axis=1, keepdims=True)
    loss[...] = parts / seeds[0:1, 0:1]
    low = low_grad[...]
    at = own_message.shape[1] - 2 * units
    value = nn(own_message[:, at : at + rows], low)
    value = value + nn(own_message[:, at + units : at + units + rows], near)
    value = (value * gate[...]).astype(BF16)
    low_two[...] = value
    edge_two[...] = (value.astype(F32) / over(facts[0:1], gate)).astype(BF16)
    grads[...] = jnp.zeros(grads.shape, F32)
    grads[:rows, :units] = nt(low, low_hidden[...])
    grads[:rows, units:] = nt(near, low_hidden[...])


def back_two_kernel(*refs):
    count = len(refs) - 2
    blocks, (back, near) = refs[:count], refs[count:]
    near[...] = summed(blocks, lambda s, n: back[s * n : (s + 1) * n, :], nn).astype(BF16)


def back_one_kernel(peers, *refs):
    lows, nears = refs[:peers], refs[peers : 2 * peers]
    (two_turned, gate, facts, first, in_sums, input_two, grads_three) = refs[
        2 * peers : 2 * peers + 7
    ]
    (partial, whole_low, whole_near) = refs[2 * peers + 7 :]
    units = lows[0].shape[0]
    hidden = units * peers
    rows = first.shape[0]
    wide = -(-rows // 128) * 128
    mine = lax.axis_index("mp")
    for step in range(peers):
        place = pl.ds(pl.multiple_of((mine ^ step) * units, units), units)
        whole_low[place, :] = lows[step][...]
        whole_near[place, :] = nears[step][...]
    value = nn(two_turned[:, :hidden], whole_low[...])
    value = value + nn(two_turned[:, hidden:], whole_near[...])
    low = (value * gate[...]).astype(BF16)
    edge = (low.astype(F32) / over(facts[0:1], gate)).astype(BF16)
    sums = in_sums[...]
    high = sums.astype(BF16)
    rest = (sums - high.astype(F32)).astype(BF16)
    blank = jnp.zeros((units, wide - rows), F32)
    partial[:, :wide] = jnp.concatenate([nt(low, first[...]), blank], axis=1)
    partial[:, wide : 2 * wide] = jnp.concatenate([nt(edge, high) + nt(edge, rest), blank], axis=1)
    at = 2 * wide
    partial[:, at : at + hidden] = nt(lows[0][...], input_two[...])
    at += hidden
    partial[:, at : at + hidden] = nt(nears[0][...], input_two[...])
    at += hidden
    partial[:, at:] = grads_three[...]


def add_kernel(shares, out):
    total = shares[0]
    for step in range(1, shares.shape[0]):
        total = total + shares[step]
    for step in range(out.shape[0]):
        out[step] = total


def pieces_of(total, one, two, three):
    in_units, hidden = one.shape[2], two.shape[2]
    classes, units = three.shape[0], three.shape[2]
    wide = -(-in_units // 128) * 128
    at = 2 * wide + 2 * hidden
    return [
        (0, lambda ref: (ref, 0), total[:, :in_units]),
        (0, lambda ref: (ref, 1), total[:, wide : wide + in_units]),
        (1, lambda ref: (ref, 0), total[:, 2 * wide : 2 * wide + hidden]),
        (1, lambda ref: (ref, 1), total[:, 2 * wide + hidden : at]),
        (2, lambda ref: (ref, (slice(None), 0, slice(None))), total[:classes, at : at + units]),
        (2, lambda ref: (ref, (slice(None), 1, slice(None))), total[:classes, at + units :]),
    ]


def moments_kernel(total, *refs):
    weights, firsts, seconds = refs[0:3], refs[3:6], refs[6:9]
    firsts_new, seconds_new, updates = refs[9:12], refs[12:15], refs[15:18]
    squares = refs[18]
    row = lax.broadcasted_iota(jnp.int32, squares.shape, 0)
    lane = lax.broadcasted_iota(jnp.int32, squares.shape, 1)
    found = jnp.zeros(squares.shape, F32)
    for place, (which, at, grad) in enumerate(pieces_of(total[...], *weights)):
        index = at(None)[1]
        weight = weights[which][index]
        parts = lamb_parts(weight, firsts[which][index], seconds[which][index], grad)
        firsts_new[which][index] = parts[0]
        seconds_new[which][index] = parts[1]
        updates[which][index] = parts[2]
        for line, value in ((0, weight), (1, parts[2])):
            square = jnp.sum(value * value, axis=0, keepdims=True)
            square = jnp.sum(square, axis=1, keepdims=True)
            here = jnp.where(row == line, jnp.where(lane == place, 1.0, 0.0), 0.0)
            found = found + here * over(square, found)
    squares[...] = found


def steps_kernel(squares, *refs):
    weights, updates = refs[0:3], refs[3:6]
    news, copies, norms = refs[6:9], refs[9:12], refs[12]
    roots = jnp.sqrt(squares[...])
    norms[...] = roots
    for place in range(6):
        which = place // 2
        index = (slice(None), place % 2, slice(None)) if which == 2 else place % 2
        ratio = roots[0:1, place : place + 1] / roots[1:2, place : place + 1]
        weight = weights[which][index]
        new = weight - 0.5 * over(ratio, weight) * updates[which][index]
        news[which][index] = new
        copies[which][index] = new.astype(BF16)


def local_direct(
    features,
    edge_dst,
    degree,
    fresh,
    seed_mask,
    labels,
    table,
    w_one,
    w_two,
    w_three,
    m_one,
    v_one,
    m_two,
    v_two,
    m_three,
    v_three,
):
    devices = lax.axis_size("graph")
    peers = lax.axis_size("mp")
    nodes, in_units = features.shape
    fanout = edge_dst.shape[1]
    units = w_one.shape[2]
    hidden = w_two.shape[2]
    classes = w_three.shape[2]
    wide_in = -(-in_units // 128) * 128
    first_rows = -(-(in_units + 2 * fanout + 1) // 16) * 16
    class_rows = -(-(classes + 1) // 16) * 16
    line = (1, nodes)
    degree, fresh, valid, labels = [
        value.reshape(line) for value in (degree, fresh, seed_mask, labels)
    ]
    edges = edge_dst.T
    ones = [jnp.transpose(value, (0, 2, 1)) for value in (w_one, m_one, v_one)]
    twos = [w_two, m_two, v_two]
    threes = [jnp.transpose(value, (2, 0, 1)) for value in (w_three, m_three, v_three)]

    def exchange(block, axis, size):
        return [block] + [
            lax.ppermute(block, axis, [(i, i ^ step) for i in range(size)])
            for step in range(1, size)
        ]

    def gather(block):
        return exchange(block, "graph", devices)

    def gather_shared(block, beside=None):
        half = devices // 2
        got = []
        for step in range(1, half + 1):
            pairs = [
                (i * peers + j, (i ^ (step + half * (j & 1))) * peers + j)
                for i in range(devices)
                for j in range(peers)
                if step + half * (j & 1) < devices
            ]
            got.append(lax.ppermute(block, ("graph", "mp"), pairs))
        if beside is not None:
            got[-1], beside = lax.optimization_barrier((got[-1], beside))
        swaps = [(j, j ^ 1) for j in range(peers)]
        blocks = [block] + got + [lax.ppermute(part, "mp", swaps) for part in got]
        return blocks if beside is None else (blocks, beside)

    own_lanes = nodes + 2 * wide_in + 2 * hidden + 2 * units
    first, own, facts, edges, table = call(
        messages_kernel,
        [
            ((first_rows, nodes), BF16),
            ((units, own_lanes), BF16),
            ((4, nodes), F32),
            (edges.shape, jnp.int32),
            (table.shape, F32),
        ],
        features.T,
        edges,
        degree,
        fresh,
        valid,
        labels,
        table,
        ones[0],
        w_two,
        threes[0],
        held=False,
    )
    (back,) = call(back_kernel, [((devices * nodes, nodes), BF16)], edges)
    firsts, back = gather_shared(first, back)
    owns = exchange(own, "mp", peers)
    old, one, two_turned, three_turned = call(
        weights_kernel,
        [
            ((hidden, nodes), BF16),
            ((hidden, 2 * wide_in), BF16),
            ((units, 2 * hidden), BF16),
            ((2 * units, hidden), BF16),
        ],
        *owns,
        scratch=[((hidden, 2 * hidden), F32), ((hidden, 2 * units), F32)],
    )
    ahead, in_sums, gate_one, hidden_one, input_two, own_two, near_two, seeds = call(
        lambda *refs: one_kernel(in_units, fanout, *refs),
        [
            ((nodes, devices * nodes), BF16),
            ((first_rows, nodes), F32),
            ((units, nodes), F32),
            ((units, nodes), F32),
            ((hidden, nodes), BF16),
            ((units, nodes), F32),
            ((units, nodes), BF16),
            ((8, 128), F32),
        ],
        *firsts,
        facts,
        table,
        old,
        one,
        own,
        scratch=[((hidden, nodes), F32), ((devices, first_rows, nodes), BF16)],
    )
    table_new, low_hidden, gate_two = call(
        two_kernel,
        [((2, units, nodes), F32), ((units, nodes), BF16), ((units, nodes), F32)],
        *gather(near_two),
        ahead,
        own_two,
        facts,
        table,
        hidden_one,
    )
    own_three, near_three = call(
        three_kernel,
        [((class_rows, nodes), F32), ((class_rows, nodes), BF16)],
        *exchange(low_hidden, "mp", peers),
        three_turned,
        scratch=[((hidden, nodes), BF16)],
    )
    low_three, message = call(
        lambda *refs: loss_kernel(classes, *refs),
        [((class_rows, nodes), BF16), ((class_rows, nodes), BF16)],
        *gather_shared(near_three),
        ahead,
        own_three,
        facts,
        seeds,
        scratch=[((devices, class_rows, nodes), BF16)],
    )
    loss, grads_three, low_two, edge_two = call(
        lambda *refs: back_three_kernel(classes, *refs),
        [
            ((1, 1), F32, 0),
            ((units, 2 * units), F32),
            ((units, nodes), BF16),
            ((units, nodes), BF16),
        ],
        *gather_shared(message),
        back,
        low_three,
        low_hidden,
        own,
        gate_two,
        facts,
        seeds,
        scratch=[((devices, class_rows, nodes), BF16)],
    )
    edges_two = gather(edge_two)
    lows = exchange(low_two, "mp", peers)
    (near_grad,) = call(back_two_kernel, [((units, nodes), BF16)], *edges_two, back)
    nears = exchange(near_grad, "mp", peers)
    lanes = 2 * wide_in + 2 * hidden + 2 * units
    (partial,) = call(
        lambda *refs: back_one_kernel(peers, *refs),
        [((units, lanes), F32)],
        *lows,
        *nears,
        two_turned,
        gate_one,
        facts,
        first,
        in_sums,
        input_two,
        grads_three,
        scratch=[((hidden, nodes), BF16)] * 2,
    )

    share = partial.reshape(devices, units // devices, lanes)
    share = lax.all_to_all(share, "graph", 0, 0)
    (share,) = call(add_kernel, [(share.shape, F32)], share)
    total = lax.all_to_all(share, "graph", 0, 0).reshape(units, lanes)
    shapes = [(value.shape, F32) for value in (ones[0], w_two, threes[0])]
    found = call(
        moments_kernel,
        [shape + (0,) for shape in shapes * 2] + shapes + [((2, 6), F32)],
        total,
        *(group[0] for group in (ones, twos, threes)),
        *(group[1] for group in (ones, twos, threes)),
        *(group[2] for group in (ones, twos, threes)),
    )
    found_norms = lax.psum(found[9], "mp")
    stepped = call(
        steps_kernel,
        [(shape, F32, 0) for shape, kind in shapes]
        + [(shape, BF16, 0) for shape, kind in shapes]
        + [((2, 6), F32, 0)],
        found_norms,
        ones[0],
        w_two,
        threes[0],
        *found[6:9],
    )

    def restored(values):
        return (
            jnp.transpose(values[0], (0, 2, 1)),
            values[1],
            jnp.transpose(values[2], (1, 2, 0)),
        )

    return (
        loss.reshape(()),
        *restored(stepped[0:3]),
        *restored(stepped[3:6]),
        *restored(found[0:3]),
        *restored(found[3:6]),
        stepped[6],
        table_new,
    )


def local_wide(
    features,
    edge_dst,
    degree,
    fresh,
    seed_mask,
    labels,
    table,
    w_one,
    w_two,
    w_three,
    m_one,
    v_one,
    m_two,
    v_two,
    m_three,
    v_three,
):
    devices = lax.axis_size("graph")
    me = lax.axis_index("graph")
    mine = lax.axis_index("mp")
    nodes, in_units = features.shape
    fanout = edge_dst.shape[1]
    units = w_one.shape[2]
    hidden = w_two.shape[2]
    classes = w_three.shape[2]
    degrees = degree.astype(F32)[None, :]
    is_fresh = (fresh > 0)[None, :]
    valid = seed_mask.astype(F32)[None, :]

    def gather(block):
        return lax.all_gather(block, "graph", axis=1, tiled=True)

    dst_rows = edge_dst.T
    feature_rows = features.T
    first_rows = in_units + 2 * fanout + 1
    first_message = pad_rows(
        jnp.concatenate(
            [
                feature_rows,
                (dst_rows // DIGIT).astype(BF16),
                (dst_rows % DIGIT).astype(BF16),
                valid.astype(BF16),
            ],
            axis=0,
        ),
        -(-first_rows // 16) * 16,
    )
    firsts = gather(first_message)
    low_one = jnp.transpose(w_one.astype(BF16), (0, 2, 1))
    low_two = w_two.astype(BF16)
    low_three = w_three.astype(BF16)
    wide_in = -(-in_units // 128) * 128
    wide_class = -(-classes // 64) * 64
    own_message = jnp.concatenate(
        [
            table[0].astype(BF16),
            pad_lanes(low_one[0], wide_in),
            pad_lanes(low_one[1], wide_in),
            low_two[0],
            low_two[1],
            pad_lanes(low_three[0], wide_class),
            pad_lanes(low_three[1], wide_class),
        ],
        axis=1,
    )
    whole = lax.all_gather(own_message, "mp", axis=0, tiled=True)
    cuts = [nodes, wide_in, wide_in, hidden, hidden, wide_class, wide_class]
    pieces = []
    at = 0
    for cut in cuts:
        pieces.append(whole[:, at : at + cut])
        at += cut
    old_one, all_one_self, all_one_near = pieces[0], pieces[1][:, :in_units], pieces[2][:, :in_units]
    all_two_self, all_two_near = pieces[3], pieces[4]
    all_three_self, all_three_near = pieces[5][:, :classes], pieces[6][:, :classes]

    all_features = firsts[:in_units]
    high = firsts[in_units : in_units + fanout].astype(F32)
    low = firsts[in_units + fanout : in_units + 2 * fanout].astype(F32)
    all_dst = (high * DIGIT + low).astype(jnp.int32)
    seed_count = jnp.sum(firsts[in_units + 2 * fanout].astype(F32))

    def spread(all_rows):
        def step(total, block):
            rows = lax.dynamic_slice_in_dim(all_rows, block * nodes, nodes, 1)
            dst = lax.dynamic_slice_in_dim(all_dst, block * nodes, nodes, 1)
            return total + nt(rows, count_block(dst, me * nodes, nodes)), None

        start = jnp.zeros((all_rows.shape[0], nodes), F32)
        return lax.scan(step, start, jnp.arange(devices, dtype=jnp.int32))[0]

    def collect(all_rows):
        def step(total, block):
            rows = lax.dynamic_slice_in_dim(all_rows, block * nodes, nodes, 1)
            return total + nn(rows, count_block(dst_rows, block * nodes, nodes)), None

        start = jnp.zeros((all_rows.shape[0], nodes), F32)
        return lax.scan(step, start, jnp.arange(devices, dtype=jnp.int32))[0]

    def mine_of(rows):
        return lax.dynamic_slice_in_dim(rows, mine * units, units, 0)

    near_one = nn(all_one_near, all_features).astype(BF16)
    in_sums = spread(all_features)
    pre_one = nn(all_one_self, feature_rows) + spread(near_one) / degrees
    input_two = jnp.where(is_fresh, jax.nn.relu(pre_one).astype(BF16), old_one)
    pre_one = mine_of(pre_one)
    hidden_one = jnp.where(is_fresh, jax.nn.relu(pre_one), table[0])
    near_two = nn(low_two[1], input_two).astype(BF16)
    pre_two = nn(low_two[0], input_two) + spread(gather(near_two)) / degrees
    hidden_two = jnp.where(is_fresh, jax.nn.relu(pre_two), table[1])
    low_hidden = hidden_two.astype(BF16)
    input_three = lax.all_gather(low_hidden, "mp", axis=0, tiled=True)
    near_three = tn(all_three_near, input_three).astype(BF16)
    class_rows = -(-(classes + 1) // 16) * 16
    sums = spread(gather(pad_rows(near_three, class_rows)))[:classes]
    logits = tn(all_three_self, input_three) + sums / degrees
    log_probs = jax.nn.log_softmax(logits, axis=0)
    targets = (lax.broadcasted_iota(jnp.int32, logits.shape, 0) == labels[None, :]).astype(F32)
    per_seed = -(
        0.9 * jnp.sum(targets * log_probs, axis=0, keepdims=True)
        + 0.1 * jnp.mean(log_probs, axis=0, keepdims=True)
    )
    loss_part = jnp.sum(per_seed * valid)

    grad_logits = valid * (jnp.exp(log_probs) - 0.9 * targets - 0.1 / classes) / seed_count
    low_grad_three = grad_logits.astype(BF16)
    edge_three = (low_grad_three.astype(F32) / degrees).astype(BF16)
    lanes = lax.broadcasted_iota(jnp.int32, (1, nodes), 1)
    loss_high = kept(loss_part)
    loss_mid = kept(loss_part - loss_high)
    loss_row = jnp.where(
        lanes == 0,
        loss_high,
        jnp.where(
            lanes == 1, loss_mid, jnp.where(lanes == 2, loss_part - loss_high - loss_mid, 0.0)
        ),
    ).astype(BF16)
    thirds = gather(pad_rows(jnp.concatenate([edge_three, loss_row], axis=0), class_rows))
    loss_value = jnp.sum(thirds[classes].astype(F32)) / seed_count
    near_grad_three = collect(thirds)[:classes].astype(BF16)
    grads_three = [nt(low_hidden, low_grad_three), nt(low_hidden, near_grad_three)]
    grad_hidden_two = nn(low_three[0], low_grad_three) + nn(low_three[1], near_grad_three)
    low_grad_two = jnp.where(is_fresh & (pre_two > 0), grad_hidden_two, 0.0).astype(BF16)
    edge_two = (low_grad_two.astype(F32) / degrees).astype(BF16)
    near_grad_two = collect(gather(edge_two)).astype(BF16)
    grads_two = [nt(low_grad_two, input_two), nt(near_grad_two, input_two)]
    both = lax.all_gather(
        jnp.concatenate([low_grad_two, near_grad_two], axis=1), "mp", axis=0, tiled=True
    )
    columns_self = lax.dynamic_slice_in_dim(all_two_self, mine * units, units, 1)
    columns_near = lax.dynamic_slice_in_dim(all_two_near, mine * units, units, 1)
    grad_hidden_one = tn(columns_self, both[:, :nodes]) + tn(columns_near, both[:, nodes:])
    low_grad_one = jnp.where(is_fresh & (pre_one > 0), grad_hidden_one, 0.0).astype(BF16)
    edge_one = (low_grad_one.astype(F32) / degrees).astype(BF16)
    sums_high, sums_low = in_two(in_sums)
    grads_one = [
        nt(low_grad_one, feature_rows),
        nt(edge_one, sums_high) + nt(edge_one, sums_low),
    ]

    partial = jnp.concatenate(
        [pad_lanes(g, wide_in) for g in grads_one]
        + grads_two
        + [pad_lanes(g, wide_class) for g in grads_three],
        axis=1,
    )
    share = partial.reshape(devices, units // devices, partial.shape[1])
    share = jnp.sum(lax.all_to_all(share, "graph", 0, 0), axis=0)
    share = jnp.broadcast_to(share[None], (devices,) + share.shape)
    total = lax.all_to_all(share, "graph", 0, 0).reshape(partial.shape)
    at = 0
    pieces = []
    for cut, use in (
        (wide_in, in_units),
        (wide_in, in_units),
        (hidden, hidden),
        (hidden, hidden),
        (wide_class, classes),
        (wide_class, classes),
    ):
        pieces.append(total[:, at : at + use])
        at += cut
    grad_one = jnp.stack([pieces[0].T, pieces[1].T])
    grad_two = jnp.stack(pieces[2:4])
    grad_three = jnp.stack(pieces[4:6])

    one_parts = lamb_parts(w_one, m_one, v_one, grad_one)
    two_parts = lamb_parts(w_two, m_two, v_two, grad_two)
    three_parts = lamb_parts(w_three, m_three, v_three, grad_three)

    def squares(values):
        return jnp.concatenate([jnp.sum(v * v, axis=(1, 2)) for v in values])

    norms = jnp.sqrt(
        lax.psum(
            jnp.stack(
                [
                    squares([w_one, w_two, w_three]),
                    squares([one_parts[2], two_parts[2], three_parts[2]]),
                ]
            ),
            "mp",
        )
    )
    ratios = (norms[0] / norms[1])[:, None, None]
    one_new = w_one - 0.5 * ratios[0:2] * one_parts[2]
    two_new = w_two - 0.5 * ratios[2:4] * two_parts[2]
    three_new = w_three - 0.5 * ratios[4:6] * three_parts[2]
    table_new = jnp.stack([hidden_one, hidden_two], axis=0)
    return (
        loss_value,
        one_new,
        two_new,
        three_new,
        one_new.astype(BF16),
        two_new.astype(BF16),
        three_new.astype(BF16),
        one_parts[0],
        two_parts[0],
        three_parts[0],
        one_parts[1],
        two_parts[1],
        three_parts[1],
        norms,
        table_new,
    )


def solution(mesh):
    in_specs = (
        P("graph", None),
        P("graph", None),
        P("graph"),
        P("graph"),
        P("graph"),
        P("graph"),
        P(None, "mp", "graph"),
        P(None, None, "mp"),
        P(None, "mp", None),
        P(None, "mp", None),
        P(None, None, "mp"),
        P(None, None, "mp"),
        P(None, "mp", None),
        P(None, "mp", None),
        P(None, "mp", None),
        P(None, "mp", None),
    )
    out_specs = (
        P(),
        P(None, None, "mp"),
        P(None, "mp", None),
        P(None, "mp", None),
        P(None, None, "mp"),
        P(None, "mp", None),
        P(None, "mp", None),
        P(None, None, "mp"),
        P(None, "mp", None),
        P(None, "mp", None),
        P(None, None, "mp"),
        P(None, "mp", None),
        P(None, "mp", None),
        P(),
        P(None, "mp", "graph"),
    )
    axes = mesh.shape["graph"], mesh.shape["mp"]
    few = axes[0] <= DIRECT_MOST and all(size > 1 and size & (size - 1) == 0 for size in axes)
    local = local_direct if few else local_wide
    return jax.shard_map(local, mesh=mesh, in_specs=in_specs, out_specs=out_specs, check_vma=False)
```

```python
import jax
import jax.numpy as jnp
from jax import lax
from jax.experimental import pallas as pl
from jax.experimental.pallas import tpu as pltpu
from jax.sharding import PartitionSpec as P

STEP = 3
F32 = jnp.float32
BF16 = jnp.bfloat16
DIGIT = 256
DIRECT_MOST = 8


def nt(left, right):
    return lax.dot_general(left, right, (((1,), (1,)), ((), ())), preferred_element_type=F32)


def nn(left, right):
    return lax.dot_general(left, right, (((1,), (0,)), ((), ())), preferred_element_type=F32)


def tn(left, right):
    return lax.dot_general(left, right, (((0,), (0,)), ((), ())), preferred_element_type=F32)


def kept(value):
    return lax.reduce_precision(value, 8, 7)


def in_two(value):
    high = kept(value)
    return high.astype(BF16), (value - high).astype(BF16)


def count_block(dst_rows, first, size):
    shape = (size, dst_rows.shape[1])
    ids = lax.broadcasted_iota(jnp.int32, shape, 0).astype(jnp.int16)
    total = None
    for slot in range(dst_rows.shape[0]):
        near = jnp.broadcast_to(dst_rows[slot : slot + 1] - first, shape).astype(jnp.int16)
        hit = jnp.where(ids == near, jnp.ones(shape, BF16), jnp.zeros(shape, BF16))
        total = hit if total is None else total + hit
    return total


def pad_rows(value, rows):
    return jnp.pad(value, ((0, rows - value.shape[0]), (0, 0)))


def pad_lanes(value, lanes):
    return jnp.pad(value, ((0, 0), (0, lanes - value.shape[1])))


def lamb_parts(weights, first, second, grad):
    correction = 1.0 - 0.5**STEP
    first_new = 0.5 * first + 0.5 * grad
    second_new = 0.5 * second + 0.5 * grad * grad
    update = first_new / correction / (jnp.sqrt(second_new / correction) + 1e-06) + 0.01 * weights
    return (first_new, second_new, update)


VMEM_BYTES = 24 * 2**20


def call(kernel, outs, *operands, scratch=(), held=True):
    place = pltpu.VMEM if held else pltpu.HBM
    operands = [pltpu.with_memory_space_constraint(value, place) for value in operands]
    space = pl.BlockSpec(memory_space=pltpu.VMEM)
    found = pl.pallas_call(
        kernel,
        out_shape=[
            jax.ShapeDtypeStruct(*out[:2]) if len(out) > 2 else pltpu.VMEM(*out) for out in outs
        ],
        in_specs=[space] * len(operands),
        out_specs=[space] * len(outs),
        scratch_shapes=[pltpu.VMEM(*each) for each in scratch],
        compiler_params=pltpu.CompilerParams(vmem_limit_bytes=VMEM_BYTES),
    )(*operands)
    return found


def over(row, value):
    return jnp.broadcast_to(row, value.shape)


def arrange(blocks, held):
    half = (len(blocks) - 1) // 2
    core = lax.axis_index("mp") & 1
    held[0] = blocks[0][...]
    for step in range(1, half):
        held[step + half * core] = blocks[step][...]
        held[step + half - half * core] = blocks[half + step][...]
    held[half] = blocks[half][...] + blocks[2 * half][...]


def messages_kernel(
    features, edges, degree, fresh, valid, labels, table, one, two, three, *outs
):
    first, own, facts, edges_kept, table_kept = outs
    for place, fact in enumerate((degree, fresh, valid, labels)):
        facts[place : place + 1] = fact[...].astype(F32)
    edges_kept[...] = edges[...]
    table_kept[...] = table[...]
    in_units, nodes = features.shape
    fanout = edges.shape[0]
    units, hidden = two.shape[1:]
    wide_in = -(-in_units // 128) * 128
    classes = three.shape[0]
    rows = first.shape[0]
    dst = edges[...]
    high = dst // DIGIT
    tail = [high, dst - high * DIGIT, valid[...]]
    used = in_units + 2 * fanout + 1
    whole = jnp.concatenate(
        [features[...].astype(F32)]
        + [part.astype(F32) for part in tail]
        + [jnp.zeros((rows - used, nodes), F32)],
        axis=0,
    )
    first[...] = whole.astype(BF16)
    own[:, :nodes] = table[0].astype(BF16)
    at = nodes
    blank = jnp.zeros((units, wide_in - in_units), F32)
    for which in range(2):
        own[:, at : at + wide_in] = jnp.concatenate([one[which], blank], axis=1).astype(BF16)
        at += wide_in
    for which in range(2):
        own[:, at : at + hidden] = two[which].astype(BF16)
        at += hidden
    pair = jnp.concatenate([three[:, 0, :], three[:, 1, :]], axis=1)
    pair = jnp.concatenate([pair, jnp.zeros((units - classes, 2 * units), F32)], axis=0).T
    turned = jnp.concatenate([pair[:units], pair[units:]], axis=1)
    own[:, at : at + 2 * units] = turned.astype(BF16)


def back_kernel(edges, back):
    nodes = edges.shape[1]
    me = lax.axis_index("graph")
    for step in range(back.shape[0] // nodes):
        counts = count_block(edges, (me ^ step) * nodes, nodes)
        back[step * nodes : (step + 1) * nodes, :] = counts


def weights_kernel(*refs):
    count = len(refs) - 6
    blocks = refs[:count]
    (old, one, two_turned, three_turned, whole_two, whole_three) = refs[count:]
    units = blocks[0].shape[0]
    mine = lax.axis_index("mp")
    nodes = old.shape[1]
    span = one.shape[1]
    hidden = whole_two.shape[1] // 2
    for step, block in enumerate(blocks):
        place = pl.ds(pl.multiple_of((mine ^ step) * units, units), units)
        old[place, :] = block[:, :nodes]
        one[place, :] = block[:, nodes : nodes + span]
        whole_two[place, :] = block[:, nodes + span : nodes + span + 2 * hidden].astype(F32)
        whole_three[place, :] = block[:, nodes + span + 2 * hidden :].astype(F32)
    three_turned[...] = whole_three[...].T.astype(BF16)
    turned = whole_two[...].T
    whole_two_turned = turned.reshape(2, hidden, hidden)
    for which in range(2):
        part = whole_two_turned[which]
        picked = part[:units]
        for step in range(1, hidden // units):
            picked = jnp.where(mine == step, part[step * units : (step + 1) * units], picked)
        two_turned[:, which * hidden : (which + 1) * hidden] = picked.astype(BF16)


def one_kernel(in_units, fanout, *refs):
    count = len(refs) - 15
    blocks = refs[:count]
    (facts, table, old, one, own) = refs[count : count + 5]
    (ahead, in_sums, gate, hidden_one, input_two, own_two, near_two, seeds) = refs[
        count + 5 : count + 13
    ]
    pre, held = refs[count + 13 :]
    nodes = facts.shape[1]
    rows = blocks[0].shape[0]
    units, hidden = own_two.shape[0], input_two.shape[0]
    me = lax.axis_index("graph")
    mine = lax.axis_index("mp")
    wide = one.shape[1] // 2
    one_self, one_near = one[:, :rows], one[:, wide : wide + rows]
    base = in_units // 16 * 16
    totals = None
    sums = None
    seed_rows = None
    arrange(blocks, held)
    for step in range(held.shape[0]):
        value = held[step]
        tail = held[step, base:, :].astype(F32)
        at = in_units - base
        digits = tail[at : at + fanout] * DIGIT + tail[at + fanout : at + 2 * fanout]
        seed_row = tail[at + 2 * fanout : at + 2 * fanout + 1]
        counts = count_block(digits.astype(jnp.int32), me * nodes, nodes)
        ahead[:, step * nodes : (step + 1) * nodes] = counts
        near = nn(one_near, value).astype(BF16)
        total, part = nt(near, counts), nt(value, counts)
        totals = total if totals is None else totals + total
        sums = part if sums is None else sums + part
        seed_rows = seed_row if seed_rows is None else seed_rows + seed_row
    in_sums[...] = sums
    seeds[...] = jnp.broadcast_to(jnp.sum(seed_rows, axis=1, keepdims=True), seeds.shape)
    value = nn(one_self, blocks[0][...]) + totals / over(facts[0:1], totals)
    pre[...] = value
    keep = over(facts[1:2], value) > 0
    inputs = jnp.where(keep, jnp.maximum(value, 0.0), old[...].astype(F32)).astype(BF16)
    input_two[...] = inputs
    mine_pre = pre[pl.ds(pl.multiple_of(mine * units, units), units), :]
    keep = over(facts[1:2], mine_pre) > 0
    hidden_one[...] = jnp.where(keep, jnp.maximum(mine_pre, 0.0), table[0])
    gate[...] = jnp.where(keep, jnp.where(mine_pre > 0, 1.0, 0.0), 0.0)
    at = nodes + 2 * wide
    own_two[...] = nn(own[:, at : at + hidden], inputs)
    near_two[...] = nn(own[:, at + hidden : at + 2 * hidden], inputs).astype(BF16)


def summed(blocks, counts, product):
    nodes = blocks[0].shape[1]
    total = None
    for step, block in enumerate(blocks):
        part = product(block[...], counts(step, nodes))
        total = part if total is None else total + part
    return total


def two_kernel(*refs):
    count = len(refs) - 8
    blocks = refs[:count]
    (ahead, own_two, facts, table, hidden_one) = refs[count : count + 5]
    (table_new, low_hidden, gate) = refs[count + 5 :]
    sums = summed(blocks, lambda s, n: ahead[:, s * n : (s + 1) * n], nt)
    value = own_two[...] + sums / over(facts[0:1], sums)
    keep = over(facts[1:2], value) > 0
    hidden = jnp.where(keep, jnp.maximum(value, 0.0), table[1])
    table_new[0] = hidden_one[...]
    table_new[1] = hidden
    low_hidden[...] = hidden.astype(BF16)
    gate[...] = jnp.where(keep, jnp.where(value > 0, 1.0, 0.0), 0.0)


def three_kernel(*refs):
    count = len(refs) - 4
    blocks, (turned, own, near, whole) = refs[:count], refs[count:]
    units = blocks[0].shape[0]
    mine = lax.axis_index("mp")
    for step, block in enumerate(blocks):
        whole[pl.ds(pl.multiple_of((mine ^ step) * units, units), units), :] = block[...]
    both = nn(turned[...], whole[...])
    rows = own.shape[0]
    own[...] = both[:rows]
    near[...] = both[turned.shape[0] // 2 : turned.shape[0] // 2 + rows].astype(BF16)


def loss_kernel(classes, *refs):
    count = len(refs) - 7
    (ahead, own, facts, seeds, low_grad, message, held) = refs[count:]
    arrange(refs[:count], held)
    blocks = [held.at[step] for step in range(held.shape[0])]
    sums = summed(blocks, lambda s, n: ahead[:, s * n : (s + 1) * n], nt)
    degrees = over(facts[0:1], sums)
    logits = own[...] + sums / degrees
    row = lax.broadcasted_iota(jnp.int32, logits.shape, 0)
    real = row < classes
    logits = jnp.where(real, logits, -1e30)
    shifted = logits - over(jnp.max(logits, axis=0, keepdims=True), logits)
    scale = jnp.log(jnp.sum(jnp.exp(shifted), axis=0, keepdims=True))
    log_probs = jnp.where(real, shifted - over(scale, logits), 0.0)
    targets = jnp.where(row.astype(F32) == over(facts[3:4], logits), 1.0, 0.0)
    chosen = jnp.sum(targets * log_probs, axis=0, keepdims=True)
    per_seed = -(0.9 * chosen + 0.1 * (jnp.sum(log_probs, axis=0, keepdims=True) / classes))
    weight = facts[2:3]
    loss = jnp.sum(per_seed * weight, axis=1, keepdims=True)
    total = over(seeds[0:1, 0:1], logits)
    grad = over(weight, logits) * (jnp.exp(log_probs) - 0.9 * targets - 0.1 / classes) / total
    low = jnp.where(real, grad, 0.0).astype(BF16)
    low_grad[...] = low
    edge = low.astype(F32) / degrees
    lane = lax.broadcasted_iota(jnp.int32, logits.shape, 1)
    high = loss.astype(BF16).astype(F32)
    middle = (loss - high).astype(BF16).astype(F32)
    rest = loss - high - middle
    digits = jnp.where(
        lane == 0,
        over(high, logits),
        jnp.where(lane == 1, over(middle, logits), jnp.where(lane == 2, over(rest, logits), 0.0)),
    )
    message[...] = jnp.where(real, edge, jnp.where(row == classes, digits, 0.0)).astype(BF16)


def back_three_kernel(classes, *refs):
    count = len(refs) - 12
    (back, low_grad, low_hidden, own_message, gate, facts, seeds) = refs[count : count + 7]
    (loss, grads, low_two, edge_two, held) = refs[count + 7 :]
    arrange(refs[:count], held)
    blocks = [held.at[step] for step in range(held.shape[0])]
    rows = blocks[0].shape[0]
    units = low_hidden.shape[0]
    sums = summed(blocks, lambda s, n: back[s * n : (s + 1) * n, :], nn)
    near = sums.astype(BF16)
    base = classes // 16 * 16
    tail = None
    for block in blocks:
        part = block[base:, :].astype(F32)
        tail = part if tail is None else tail + part
    parts = jnp.sum(tail[classes - base : classes - base + 1, :128], axis=1, keepdims=True)
    loss[...] = parts / seeds[0:1, 0:1]
    low = low_grad[...]
    at = own_message.shape[1] - 2 * units
    value = nn(own_message[:, at : at + rows], low)
    value = value + nn(own_message[:, at + units : at + units + rows], near)
    value = (value * gate[...]).astype(BF16)
    low_two[...] = value
    edge_two[...] = (value.astype(F32) / over(facts[0:1], gate)).astype(BF16)
    grads[...] = jnp.zeros(grads.shape, F32)
    grads[:rows, :units] = nt(low, low_hidden[...])
    grads[:rows, units:] = nt(near, low_hidden[...])


def back_two_kernel(*refs):
    count = len(refs) - 2
    blocks, (back, near) = refs[:count], refs[count:]
    near[...] = summed(blocks, lambda s, n: back[s * n : (s + 1) * n, :], nn).astype(BF16)


def back_one_kernel(peers, *refs):
    lows, nears = refs[:peers], refs[peers : 2 * peers]
    (two_turned, gate, facts, first, in_sums, input_two, grads_three) = refs[
        2 * peers : 2 * peers + 7
    ]
    (partial, whole_low, whole_near) = refs[2 * peers + 7 :]
    units = lows[0].shape[0]
    hidden = units * peers
    rows = first.shape[0]
    wide = -(-rows // 128) * 128
    mine = lax.axis_index("mp")
    for step in range(peers):
        place = pl.ds(pl.multiple_of((mine ^ step) * units, units), units)
        whole_low[place, :] = lows[step][...]
        whole_near[place, :] = nears[step][...]
    value = nn(two_turned[:, :hidden], whole_low[...])
    value = value + nn(two_turned[:, hidden:], whole_near[...])
    low = (value * gate[...]).astype(BF16)
    edge = (low.astype(F32) / over(facts[0:1], gate)).astype(BF16)
    sums = in_sums[...]
    high = sums.astype(BF16)
    rest = (sums - high.astype(F32)).astype(BF16)
    blank = jnp.zeros((units, wide - rows), F32)
    partial[:, :wide] = jnp.concatenate([nt(low, first[...]), blank], axis=1)
    partial[:, wide : 2 * wide] = jnp.concatenate([nt(edge, high) + nt(edge, rest), blank], axis=1)
    at = 2 * wide
    partial[:, at : at + hidden] = nt(lows[0][...], input_two[...])
    at += hidden
    partial[:, at : at + hidden] = nt(nears[0][...], input_two[...])
    at += hidden
    partial[:, at:] = grads_three[...]


def add_kernel(shares, out):
    total = shares[0]
    for step in range(1, shares.shape[0]):
        total = total + shares[step]
    for step in range(out.shape[0]):
        out[step] = total


def pieces_of(total, one, two, three):
    in_units, hidden = one.shape[2], two.shape[2]
    classes, units = three.shape[0], three.shape[2]
    wide = -(-in_units // 128) * 128
    at = 2 * wide + 2 * hidden
    return [
        (0, lambda ref: (ref, 0), total[:, :in_units]),
        (0, lambda ref: (ref, 1), total[:, wide : wide + in_units]),
        (1, lambda ref: (ref, 0), total[:, 2 * wide : 2 * wide + hidden]),
        (1, lambda ref: (ref, 1), total[:, 2 * wide + hidden : at]),
        (2, lambda ref: (ref, (slice(None), 0, slice(None))), total[:classes, at : at + units]),
        (2, lambda ref: (ref, (slice(None), 1, slice(None))), total[:classes, at + units :]),
    ]


def moments_kernel(total, *refs):
    weights, firsts, seconds = refs[0:3], refs[3:6], refs[6:9]
    firsts_new, seconds_new, updates = refs[9:12], refs[12:15], refs[15:18]
    squares = refs[18]
    row = lax.broadcasted_iota(jnp.int32, squares.shape, 0)
    lane = lax.broadcasted_iota(jnp.int32, squares.shape, 1)
    found = jnp.zeros(squares.shape, F32)
    for place, (which, at, grad) in enumerate(pieces_of(total[...], *weights)):
        index = at(None)[1]
        weight = weights[which][index]
        parts = lamb_parts(weight, firsts[which][index], seconds[which][index], grad)
        firsts_new[which][index] = parts[0]
        seconds_new[which][index] = parts[1]
        updates[which][index] = parts[2]
        for line, value in ((0, weight), (1, parts[2])):
            square = jnp.sum(value * value, axis=0, keepdims=True)
            square = jnp.sum(square, axis=1, keepdims=True)
            here = jnp.where(row == line, jnp.where(lane == place, 1.0, 0.0), 0.0)
            found = found + here * over(square, found)
    squares[...] = found


def steps_kernel(squares, *refs):
    weights, updates = refs[0:3], refs[3:6]
    news, copies, norms = refs[6:9], refs[9:12], refs[12]
    roots = jnp.sqrt(squares[...])
    norms[...] = roots
    for place in range(6):
        which = place // 2
        index = (slice(None), place % 2, slice(None)) if which == 2 else place % 2
        ratio = roots[0:1, place : place + 1] / roots[1:2, place : place + 1]
        weight = weights[which][index]
        new = weight - 0.5 * over(ratio, weight) * updates[which][index]
        news[which][index] = new
        copies[which][index] = new.astype(BF16)


def local_direct(
    features,
    edge_dst,
    degree,
    fresh,
    seed_mask,
    labels,
    table,
    w_one,
    w_two,
    w_three,
    m_one,
    v_one,
    m_two,
    v_two,
    m_three,
    v_three,
):
    devices = lax.axis_size("graph")
    peers = lax.axis_size("mp")
    nodes, in_units = features.shape
    fanout = edge_dst.shape[1]
    units = w_one.shape[2]
    hidden = w_two.shape[2]
    classes = w_three.shape[2]
    wide_in = -(-in_units // 128) * 128
    first_rows = -(-(in_units + 2 * fanout + 1) // 16) * 16
    class_rows = -(-(classes + 1) // 16) * 16
    line = (1, nodes)
    degree, fresh, valid, labels = [
        value.reshape(line) for value in (degree, fresh, seed_mask, labels)
    ]
    edges = edge_dst.T
    ones = [jnp.transpose(value, (0, 2, 1)) for value in (w_one, m_one, v_one)]
    twos = [w_two, m_two, v_two]
    threes = [jnp.transpose(value, (2, 0, 1)) for value in (w_three, m_three, v_three)]

    def exchange(block, axis, size):
        return [block] + [
            lax.ppermute(block, axis, [(i, i ^ step) for i in range(size)])
            for step in range(1, size)
        ]

    def gather(block):
        return exchange(block, "graph", devices)

    def gather_shared(block, beside=None):
        half = devices // 2
        got = []
        for step in range(1, half + 1):
            pairs = [
                (i * peers + j, (i ^ (step + half * (j & 1))) * peers + j)
                for i in range(devices)
                for j in range(peers)
                if step + half * (j & 1) < devices
            ]
            got.append(lax.ppermute(block, ("graph", "mp"), pairs))
        if beside is not None:
            got[-1], beside = lax.optimization_barrier((got[-1], beside))
        swaps = [(j, j ^ 1) for j in range(peers)]
        blocks = [block] + got + [lax.ppermute(part, "mp", swaps) for part in got]
        return blocks if beside is None else (blocks, beside)

    own_lanes = nodes + 2 * wide_in + 2 * hidden + 2 * units
    first, own, facts, edges, table = call(
        messages_kernel,
        [
            ((first_rows, nodes), BF16),
            ((units, own_lanes), BF16),
            ((4, nodes), F32),
            (edges.shape, jnp.int32),
            (table.shape, F32),
        ],
        features.T,
        edges,
        degree,
        fresh,
        valid,
        labels,
        table,
        ones[0],
        w_two,
        threes[0],
        held=False,
    )
    (back,) = call(back_kernel, [((devices * nodes, nodes), BF16)], edges)
    firsts, back = gather_shared(first, back)
    owns = exchange(own, "mp", peers)
    old, one, two_turned, three_turned = call(
        weights_kernel,
        [
            ((hidden, nodes), BF16),
            ((hidden, 2 * wide_in), BF16),
            ((units, 2 * hidden), BF16),
            ((2 * units, hidden), BF16),
        ],
        *owns,
        scratch=[((hidden, 2 * hidden), F32), ((hidden, 2 * units), F32)],
    )
    ahead, in_sums, gate_one, hidden_one, input_two, own_two, near_two, seeds = call(
        lambda *refs: one_kernel(in_units, fanout, *refs),
        [
            ((nodes, devices * nodes), BF16),
            ((first_rows, nodes), F32),
            ((units, nodes), F32),
            ((units, nodes), F32),
            ((hidden, nodes), BF16),
            ((units, nodes), F32),
            ((units, nodes), BF16),
            ((8, 128), F32),
        ],
        *firsts,
        facts,
        table,
        old,
        one,
        own,
        scratch=[((hidden, nodes), F32), ((devices, first_rows, nodes), BF16)],
    )
    table_new, low_hidden, gate_two = call(
        two_kernel,
        [((2, units, nodes), F32), ((units, nodes), BF16), ((units, nodes), F32)],
        *gather(near_two),
        ahead,
        own_two,
        facts,
        table,
        hidden_one,
    )
    own_three, near_three = call(
        three_kernel,
        [((class_rows, nodes), F32), ((class_rows, nodes), BF16)],
        *exchange(low_hidden, "mp", peers),
        three_turned,
        scratch=[((hidden, nodes), BF16)],
    )
    low_three, message = call(
        lambda *refs: loss_kernel(classes, *refs),
        [((class_rows, nodes), BF16), ((class_rows, nodes), BF16)],
        *gather_shared(near_three),
        ahead,
        own_three,
        facts,
        seeds,
        scratch=[((devices, class_rows, nodes), BF16)],
    )
    loss, grads_three, low_two, edge_two = call(
        lambda *refs: back_three_kernel(classes, *refs),
        [
            ((1, 1), F32, 0),
            ((units, 2 * units), F32),
            ((units, nodes), BF16),
            ((units, nodes), BF16),
        ],
        *gather_shared(message),
        back,
        low_three,
        low_hidden,
        own,
        gate_two,
        facts,
        seeds,
        scratch=[((devices, class_rows, nodes), BF16)],
    )
    edges_two = gather(edge_two)
    lows = exchange(low_two, "mp", peers)
    (near_grad,) = call(back_two_kernel, [((units, nodes), BF16)], *edges_two, back)
    nears = exchange(near_grad, "mp", peers)
    lanes = 2 * wide_in + 2 * hidden + 2 * units
    (partial,) = call(
        lambda *refs: back_one_kernel(peers, *refs),
        [((units, lanes), F32)],
        *lows,
        *nears,
        two_turned,
        gate_one,
        facts,
        first,
        in_sums,
        input_two,
        grads_three,
        scratch=[((hidden, nodes), BF16)] * 2,
    )

    share = partial.reshape(devices, units // devices, lanes)
    share = lax.all_to_all(share, "graph", 0, 0)
    (share,) = call(add_kernel, [(share.shape, F32)], share)
    total = lax.all_to_all(share, "graph", 0, 0).reshape(units, lanes)
    shapes = [(value.shape, F32) for value in (ones[0], w_two, threes[0])]
    found = call(
        moments_kernel,
        [shape + (0,) for shape in shapes * 2] + shapes + [((2, 6), F32)],
        total,
        *(group[0] for group in (ones, twos, threes)),
        *(group[1] for group in (ones, twos, threes)),
        *(group[2] for group in (ones, twos, threes)),
    )
    found_norms = lax.psum(found[9], "mp")
    stepped = call(
        steps_kernel,
        [(shape, F32, 0) for shape, kind in shapes]
        + [(shape, BF16, 0) for shape, kind in shapes]
        + [((2, 6), F32, 0)],
        found_norms,
        ones[0],
        w_two,
        threes[0],
        *found[6:9],
    )

    def restored(values):
        return (
            jnp.transpose(values[0], (0, 2, 1)),
            values[1],
            jnp.transpose(values[2], (1, 2, 0)),
        )

    return (
        loss.reshape(()),
        *restored(stepped[0:3]),
        *restored(stepped[3:6]),
        *restored(found[0:3]),
        *restored(found[3:6]),
        stepped[6],
        table_new,
    )


def local_wide(
    features,
    edge_dst,
    degree,
    fresh,
    seed_mask,
    labels,
    table,
    w_one,
    w_two,
    w_three,
    m_one,
    v_one,
    m_two,
    v_two,
    m_three,
    v_three,
):
    devices = lax.axis_size("graph")
    me = lax.axis_index("graph")
    mine = lax.axis_index("mp")
    nodes, in_units = features.shape
    fanout = edge_dst.shape[1]
    units = w_one.shape[2]
    hidden = w_two.shape[2]
    classes = w_three.shape[2]
    degrees = degree.astype(F32)[None, :]
    is_fresh = (fresh > 0)[None, :]
    valid = seed_mask.astype(F32)[None, :]

    def gather(block):
        return lax.all_gather(block, "graph", axis=1, tiled=True)

    dst_rows = edge_dst.T
    feature_rows = features.T
    first_rows = in_units + 2 * fanout + 1
    first_message = pad_rows(
        jnp.concatenate(
            [
                feature_rows,
                (dst_rows // DIGIT).astype(BF16),
                (dst_rows % DIGIT).astype(BF16),
                valid.astype(BF16),
            ],
            axis=0,
        ),
        -(-first_rows // 16) * 16,
    )
    firsts = gather(first_message)
    low_one = jnp.transpose(w_one.astype(BF16), (0, 2, 1))
    low_two = w_two.astype(BF16)
    low_three = w_three.astype(BF16)
    wide_in = -(-in_units // 128) * 128
    wide_class = -(-classes // 64) * 64
    own_message = jnp.concatenate(
        [
            table[0].astype(BF16),
            pad_lanes(low_one[0], wide_in),
            pad_lanes(low_one[1], wide_in),
            low_two[0],
            low_two[1],
            pad_lanes(low_three[0], wide_class),
            pad_lanes(low_three[1], wide_class),
        ],
        axis=1,
    )
    whole = lax.all_gather(own_message, "mp", axis=0, tiled=True)
    cuts = [nodes, wide_in, wide_in, hidden, hidden, wide_class, wide_class]
    pieces = []
    at = 0
    for cut in cuts:
        pieces.append(whole[:, at : at + cut])
        at += cut
    old_one, all_one_self, all_one_near = pieces[0], pieces[1][:, :in_units], pieces[2][:, :in_units]
    all_two_self, all_two_near = pieces[3], pieces[4]
    all_three_self, all_three_near = pieces[5][:, :classes], pieces[6][:, :classes]

    all_features = firsts[:in_units]
    high = firsts[in_units : in_units + fanout].astype(F32)
    low = firsts[in_units + fanout : in_units + 2 * fanout].astype(F32)
    all_dst = (high * DIGIT + low).astype(jnp.int32)
    seed_count = jnp.sum(firsts[in_units + 2 * fanout].astype(F32))

    def spread(all_rows):
        def step(total, block):
            rows = lax.dynamic_slice_in_dim(all_rows, block * nodes, nodes, 1)
            dst = lax.dynamic_slice_in_dim(all_dst, block * nodes, nodes, 1)
            return total + nt(rows, count_block(dst, me * nodes, nodes)), None

        start = jnp.zeros((all_rows.shape[0], nodes), F32)
        return lax.scan(step, start, jnp.arange(devices, dtype=jnp.int32))[0]

    def collect(all_rows):
        def step(total, block):
            rows = lax.dynamic_slice_in_dim(all_rows, block * nodes, nodes, 1)
            return total + nn(rows, count_block(dst_rows, block * nodes, nodes)), None

        start = jnp.zeros((all_rows.shape[0], nodes), F32)
        return lax.scan(step, start, jnp.arange(devices, dtype=jnp.int32))[0]

    def mine_of(rows):
        return lax.dynamic_slice_in_dim(rows, mine * units, units, 0)

    near_one = nn(all_one_near, all_features).astype(BF16)
    in_sums = spread(all_features)
    pre_one = nn(all_one_self, feature_rows) + spread(near_one) / degrees
    input_two = jnp.where(is_fresh, jax.nn.relu(pre_one).astype(BF16), old_one)
    pre_one = mine_of(pre_one)
    hidden_one = jnp.where(is_fresh, jax.nn.relu(pre_one), table[0])
    near_two = nn(low_two[1], input_two).astype(BF16)
    pre_two = nn(low_two[0], input_two) + spread(gather(near_two)) / degrees
    hidden_two = jnp.where(is_fresh, jax.nn.relu(pre_two), table[1])
    low_hidden = hidden_two.astype(BF16)
    input_three = lax.all_gather(low_hidden, "mp", axis=0, tiled=True)
    near_three = tn(all_three_near, input_three).astype(BF16)
    class_rows = -(-(classes + 1) // 16) * 16
    sums = spread(gather(pad_rows(near_three, class_rows)))[:classes]
    logits = tn(all_three_self, input_three) + sums / degrees
    log_probs = jax.nn.log_softmax(logits, axis=0)
    targets = (lax.broadcasted_iota(jnp.int32, logits.shape, 0) == labels[None, :]).astype(F32)
    per_seed = -(
        0.9 * jnp.sum(targets * log_probs, axis=0, keepdims=True)
        + 0.1 * jnp.mean(log_probs, axis=0, keepdims=True)
    )
    loss_part = jnp.sum(per_seed * valid)

    grad_logits = valid * (jnp.exp(log_probs) - 0.9 * targets - 0.1 / classes) / seed_count
    low_grad_three = grad_logits.astype(BF16)
    edge_three = (low_grad_three.astype(F32) / degrees).astype(BF16)
    lanes = lax.broadcasted_iota(jnp.int32, (1, nodes), 1)
    loss_high = kept(loss_part)
    loss_mid = kept(loss_part - loss_high)
    loss_row = jnp.where(
        lanes == 0,
        loss_high,
        jnp.where(
            lanes == 1, loss_mid, jnp.where(lanes == 2, loss_part - loss_high - loss_mid, 0.0)
        ),
    ).astype(BF16)
    thirds = gather(pad_rows(jnp.concatenate([edge_three, loss_row], axis=0), class_rows))
    loss_value = jnp.sum(thirds[classes].astype(F32)) / seed_count
    near_grad_three = collect(thirds)[:classes].astype(BF16)
    grads_three = [nt(low_hidden, low_grad_three), nt(low_hidden, near_grad_three)]
    grad_hidden_two = nn(low_three[0], low_grad_three) + nn(low_three[1], near_grad_three)
    low_grad_two = jnp.where(is_fresh & (pre_two > 0), grad_hidden_two, 0.0).astype(BF16)
    edge_two = (low_grad_two.astype(F32) / degrees).astype(BF16)
    near_grad_two = collect(gather(edge_two)).astype(BF16)
    grads_two = [nt(low_grad_two, input_two), nt(near_grad_two, input_two)]
    both = lax.all_gather(
        jnp.concatenate([low_grad_two, near_grad_two], axis=1), "mp", axis=0, tiled=True
    )
    columns_self = lax.dynamic_slice_in_dim(all_two_self, mine * units, units, 1)
    columns_near = lax.dynamic_slice_in_dim(all_two_near, mine * units, units, 1)
    grad_hidden_one = tn(columns_self, both[:, :nodes]) + tn(columns_near, both[:, nodes:])
    low_grad_one = jnp.where(is_fresh & (pre_one > 0), grad_hidden_one, 0.0).astype(BF16)
    edge_one = (low_grad_one.astype(F32) / degrees).astype(BF16)
    sums_high, sums_low = in_two(in_sums)
    grads_one = [
        nt(low_grad_one, feature_rows),
        nt(edge_one, sums_high) + nt(edge_one, sums_low),
    ]

    partial = jnp.concatenate(
        [pad_lanes(g, wide_in) for g in grads_one]
        + grads_two
        + [pad_lanes(g, wide_class) for g in grads_three],
        axis=1,
    )
    share = partial.reshape(devices, units // devices, partial.shape[1])
    share = jnp.sum(lax.all_to_all(share, "graph", 0, 0), axis=0)
    share = jnp.broadcast_to(share[None], (devices,) + share.shape)
    total = lax.all_to_all(share, "graph", 0, 0).reshape(partial.shape)
    at = 0
    pieces = []
    for cut, use in (
        (wide_in, in_units),
        (wide_in, in_units),
        (hidden, hidden),
        (hidden, hidden),
        (wide_class, classes),
        (wide_class, classes),
    ):
        pieces.append(total[:, at : at + use])
        at += cut
    grad_one = jnp.stack([pieces[0].T, pieces[1].T])
    grad_two = jnp.stack(pieces[2:4])
    grad_three = jnp.stack(pieces[4:6])

    one_parts = lamb_parts(w_one, m_one, v_one, grad_one)
    two_parts = lamb_parts(w_two, m_two, v_two, grad_two)
    three_parts = lamb_parts(w_three, m_three, v_three, grad_three)

    def squares(values):
        return jnp.concatenate([jnp.sum(v * v, axis=(1, 2)) for v in values])

    norms = jnp.sqrt(
        lax.psum(
            jnp.stack(
                [
                    squares([w_one, w_two, w_three]),
                    squares([one_parts[2], two_parts[2], three_parts[2]]),
                ]
            ),
            "mp",
        )
    )
    ratios = (norms[0] / norms[1])[:, None, None]
    one_new = w_one - 0.5 * ratios[0:2] * one_parts[2]
    two_new = w_two - 0.5 * ratios[2:4] * two_parts[2]
    three_new = w_three - 0.5 * ratios[4:6] * three_parts[2]
    table_new = jnp.stack([hidden_one, hidden_two], axis=0)
    return (
        loss_value,
        one_new,
        two_new,
        three_new,
        one_new.astype(BF16),
        two_new.astype(BF16),
        three_new.astype(BF16),
        one_parts[0],
        two_parts[0],
        three_parts[0],
        one_parts[1],
        two_parts[1],
        three_parts[1],
        norms,
        table_new,
    )


def solution(mesh):
    in_specs = (
        P("graph", None),
        P("graph", None),
        P("graph"),
        P("graph"),
        P("graph"),
        P("graph"),
        P(None, "mp", "graph"),
        P(None, None, "mp"),
        P(None, "mp", None),
        P(None, "mp", None),
        P(None, None, "mp"),
        P(None, None, "mp"),
        P(None, "mp", None),
        P(None, "mp", None),
        P(None, "mp", None),
        P(None, "mp", None),
    )
    out_specs = (
        P(),
        P(None, None, "mp"),
        P(None, "mp", None),
        P(None, "mp", None),
        P(None, None, "mp"),
        P(None, "mp", None),
        P(None, "mp", None),
        P(None, None, "mp"),
        P(None, "mp", None),
        P(None, "mp", None),
        P(None, None, "mp"),
        P(None, "mp", None),
        P(None, "mp", None),
        P(),
        P(None, "mp", "graph"),
    )
    axes = mesh.shape["graph"], mesh.shape["mp"]
    few = axes[0] <= DIRECT_MOST and all(size > 1 and size & (size - 1) == 0 for size in axes)
    local = local_direct if few else local_wide
    return jax.shard_map(local, mesh=mesh, in_specs=in_specs, out_specs=out_specs, check_vma=False)
```
